32 devices in a mesh: tm: 16 (over z, y, x), space: 2 (over core).
Axes of the slice: x: 2, y: 2, z: 4, core: 2. Of those that a mesh axis runs over, the one named last changes fastest.
Arguments:
- density: float32 [16, 256, 256], P('tm', 'space'), may hold values from 0.2 to 2
- flux_x: float32 [16, 256, 256], P('tm', 'space'), may hold values from -6 to 6
- flux_y: float32 [16, 256, 256], P('tm', 'space'), may hold values from -6 to 6
Outputs:
- density_out: float32 [16, 256, 256], P('tm', 'space')
- flux_x_out: float32 [16, 256, 256], P('tm', 'space')
- flux_y_out: float32 [16, 256, 256], P('tm', 'space')
The draws below stay inside these ranges and needn't reach their ends.
All inputs are finite; a program needn't handle non-finite values.
Results may differ from the reference program's by a relative error of at most 0.0004.
Values sent between devices are 32-bit elements; how exact they have to be, the bound alone decides.
A program may use at most 64 MiB of HBM per device.

```python
import math
import jax
import jax.numpy as jnp
from jax import lax

NS = 256
NEWTON = 4
NT = 16


def draw_density(key, part):
    logs = jax.random.uniform(key, (NT, NS, NS), jnp.float32, math.log(0.2), math.log(2.0))
    return jnp.clip(jnp.exp(logs), 0.2, 2.0).astype(jnp.float32)


def block_levels(own_key, dims, cuts, smallest, high):
    gain = 1.0
    for position, blocks in cuts:
        steps = jax.random.uniform(jax.random.fold_in(jax.random.fold_in(own_key, 6), position), (blocks,), jnp.float32, smallest / len(cuts), high / len(cuts))
        gain = gain * jnp.repeat(jnp.exp(steps), dims[position] // blocks).reshape((-1,) + (1,) * (len(dims) - 1 - position))
    return gain


def normal_values(own_key, shape, width, bound, cuts=(), kind=jnp.bfloat16):
    level = block_levels(own_key, shape, cuts, -0.22, 0.18) if cuts else 1.0
    drawn = jax.random.normal(own_key, shape, jnp.float32) * width * level
    return jnp.minimum(jnp.maximum(drawn, -bound), bound).astype(kind)


def setup_inputs(seed: int = 0) -> dict:
    seeds = jax.random.split(jax.random.key(seed), 4)
    density = draw_density(jax.random.fold_in(seeds[3], 71), 0)
    flux_x = normal_values(seeds[1], (NT, NS, NS), 1.0, 6.0, ((0, 16), (1, 2)), jnp.float32)
    flux_y = normal_values(seeds[2], (NT, NS, NS), 1.0, 6.0, ((0, 16), (1, 2)), jnp.float32)
    return dict(density=density, flux_x=flux_x, flux_y=flux_y)


prox_weight = 1.0
regular_shift = 0.0001
space_weight = 0.25
flux_weight = 0.5
highest = lax.Precision.HIGHEST

def kinetic_prox(density, flux_x, flux_y):
    square = flux_x * flux_x + flux_y * flux_y
    target = density + prox_weight + jnp.sqrt(square)
    for step in range(NEWTON):
        above = target + prox_weight
        value = (target - density) * above * above - 0.5 * prox_weight * square
        slope = above * (3.0 * target + prox_weight - 2.0 * density)
        target = target - value / slope
    shrink = target / (target + prox_weight)
    return (target, shrink * flux_x, shrink * flux_y)

def cosine_table(count):
    modes = jnp.arange(count).astype(jnp.float32)[:, None]
    points = jnp.arange(count).astype(jnp.float32)[None, :]
    table = jnp.cos(jnp.pi * modes * (2.0 * points + 1.0) / (2.0 * count))
    scales = jnp.where(modes == 0, jnp.sqrt(1.0 / count), jnp.sqrt(2.0 / count))
    return scales * table

def eigen_values(count):
    modes = jnp.arange(count).astype(jnp.float32)
    return 4.0 * jnp.sin(jnp.pi * modes / (2.0 * count)) ** 2

def divergence(field, axis):
    zeroed = jnp.moveaxis(field, axis, -1)
    zeroed = zeroed.at[..., -1].set(0.0)
    shifted = jnp.concatenate([jnp.zeros_like(zeroed[..., :1]), zeroed[..., :-1]], axis=-1)
    return jnp.moveaxis(zeroed - shifted, -1, axis)

def gradient(field, axis):
    moved = jnp.moveaxis(field, axis, -1)
    diffs = jnp.concatenate([moved[..., 1:] - moved[..., :-1], jnp.zeros_like(moved[..., :1])], axis=-1)
    return jnp.moveaxis(diffs, -1, axis)

def reference(density, flux_x, flux_y):
    rho, mom_x, mom_y = kinetic_prox(density, flux_x, flux_y)
    count = rho.shape[1]
    slices = rho.shape[0]
    before = jnp.concatenate([jnp.zeros_like(rho[:1]), rho[:-1]], axis=0)
    source = rho - before + flux_weight * (divergence(mom_x, 1) + divergence(mom_y, 2))
    table = cosine_table(count)
    halfway = jnp.einsum('ki,tij->tkj', table, source, precision=highest)
    modal = jnp.einsum('tkj,lj->tkl', halfway, table, precision=highest)
    lam = eigen_values(count)
    diag = 2.0 + regular_shift + space_weight * (lam[:, None] + lam[None, :])
    batch = modal.reshape(slices, count * count).T
    diag_full = jnp.broadcast_to(diag.reshape(count * count, 1), batch.shape)
    lower = -jnp.ones_like(batch)
    lower = lower.at[:, 0].set(0.0)
    upper = -jnp.ones_like(batch)
    upper = upper.at[:, -1].set(0.0)
    solved = lax.linalg.tridiagonal_solve(lower, diag_full, upper, batch[:, :, None])[:, :, 0]
    phihat = solved.T.reshape(slices, count, count)
    halfback = jnp.einsum('ki,tkl->til', table, phihat, precision=highest)
    potential = jnp.einsum('til,lj->tij', halfback, table, precision=highest)
    following = jnp.concatenate([potential[1:], jnp.zeros_like(potential[:1])], axis=0)
    density_out = rho - (potential - following)
    flux_x_out = mom_x - flux_weight * gradient(potential, 1)
    flux_y_out = mom_y - flux_weight * gradient(potential, 2)
    return (density_out, flux_x_out, flux_y_out)
```

```python
import jax
import jax.numpy as jnp
import numpy as np
from jax import lax
from jax.experimental import pallas as pl
from jax.experimental.pallas import tpu as pltpu
from jax.sharding import PartitionSpec as P

NEWTON = 4


prox_weight = 1.0
regular_shift = 0.0001
space_weight = 0.25
flux_weight = 0.5
highest = lax.Precision.HIGHEST


def swapped(block, axis, distance):
    count = lax.axis_size(axis)
    route = []
    for low in range(count):
        high = low | 1 << distance
        if high != low and high < count:
            route += [(low, high), (high, low)]
    return lax.ppermute(block, axis, route)


def shifted(array, axis, by):
    size = lax.axis_size(axis)
    pairs = [(i, i + by) for i in range(size) if 0 <= i + by < size]
    return lax.ppermute(array, axis, pairs)


def kinetic_prox(density, flux_x, flux_y):
    square = flux_x * flux_x + flux_y * flux_y
    target = density + prox_weight + jnp.sqrt(square)
    for step in range(NEWTON):
        above = target + prox_weight
        value = (target - density) * above * above - 0.5 * prox_weight * square
        slope = above * (3.0 * target + prox_weight - 2.0 * density)
        target = target - value / slope
    shrink = target / (target + prox_weight)
    return (target, shrink * flux_x, shrink * flux_y)


def cosine_table(count):
    modes = jnp.arange(count).astype(jnp.float32)[:, None]
    points = jnp.arange(count).astype(jnp.float32)[None, :]
    table = jnp.cos(jnp.pi * modes * (2.0 * points + 1.0) / (2.0 * count))
    scales = jnp.where(modes == 0, jnp.sqrt(1.0 / count), jnp.sqrt(2.0 / count))
    return scales * table


def eigen_values(count):
    modes = jnp.arange(count).astype(jnp.float32)
    return 4.0 * jnp.sin(jnp.pi * modes / (2.0 * count)) ** 2


def move_outward(stacked, bit):
    return swapped(stacked, "tm", bit)


def move_homeward(stacked, bit):
    return swapped(stacked, "tm", bit)


def butterfly(blocks, mover):
    total = lax.axis_size("tm")
    position = lax.axis_index("tm")
    bit_count = total.bit_length() - 1
    for bit in range(bit_count):
        higher = total >> bit + 1
        lowest = 1 << bit
        shaped = blocks.reshape((higher, 2, lowest) + blocks.shape[1:])
        own_bit = position >> bit & 1
        keeping = jnp.where(own_bit == 0, shaped[:, 0], shaped[:, 1])
        leaving = jnp.where(own_bit == 0, shaped[:, 1], shaped[:, 0])
        arrived = mover(leaving, bit)
        first_half = jnp.where(own_bit == 0, keeping, arrived)
        second_half = jnp.where(own_bit == 0, arrived, keeping)
        blocks = jnp.stack([first_half, second_half], axis=1).reshape(blocks.shape)
    return blocks


def per_device_xla(density, flux_x, flux_y):
    slabs = density.shape[0]
    rows_local = density.shape[1]
    count = density.shape[2]
    parts = lax.axis_size("space")
    modes_local = count // parts
    own_start = lax.axis_index("space") * rows_local
    mode_start = lax.axis_index("space") * modes_local
    rho, mom_x, mom_y = kinetic_prox(density, flux_x, flux_y)
    prior = shifted(rho[slabs - 1], "tm", 1)
    before = jnp.concatenate([prior[None], rho[:-1]], axis=0)
    zeroed = mom_y.at[:, :, count - 1].set(0.0)
    div_second = zeroed - jnp.concatenate(
        [jnp.zeros_like(zeroed[:, :, :1]), zeroed[:, :, :-1]], axis=2
    )
    partial_source = rho - before + flux_weight * div_second
    table = cosine_table(count)
    diff_table = jnp.concatenate(
        [table[:, :-1] - table[:, 1:], jnp.zeros_like(table[:, :1])], axis=1
    )
    stacked = jnp.concatenate([partial_source, flux_weight * mom_x], axis=1)
    column_modes = jnp.einsum("tij,kj->itk", stacked, table, precision=highest)
    left = lax.dynamic_slice(
        table, (0, own_start), (modes_local * lax.axis_size("space"), rows_local)
    )
    left_diff = lax.dynamic_slice(
        diff_table, (0, own_start), (modes_local * lax.axis_size("space"), rows_local)
    )
    both = jnp.concatenate([left, left_diff], axis=1)
    modal = lax.psum_scatter(
        jnp.einsum("ki,itj->ktj", both, column_modes, precision=highest),
        "space",
        scatter_dimension=0,
        tiled=True,
    )
    lam = eigen_values(count)
    lam_local = lax.dynamic_slice_in_dim(lam, mode_start, modes_local)
    coeff = 2.0 + regular_shift + space_weight * (lam_local[:, None] + lam[None, :])
    devices_tm = lax.axis_size("tm")
    position = lax.axis_index("tm")
    lines_local = modes_local * count
    line_group = lines_local // devices_tm
    steps_all = devices_tm * slabs
    outgoing = jnp.transpose(modal, (0, 2, 1)).reshape(devices_tm, line_group, slabs)
    incoming = butterfly(outgoing, move_outward)
    series = jnp.transpose(incoming, (1, 0, 2)).reshape(line_group, steps_all)
    line_coeff = lax.dynamic_slice_in_dim(
        coeff.reshape(lines_local), position * line_group, line_group
    )
    column = lax.broadcasted_iota(jnp.int32, (line_group, steps_all), 1)
    below_band = jnp.where(column == 0, 0.0, -1.0).astype(jnp.float32)
    above_band = jnp.where(column == steps_all - 1, 0.0, -1.0).astype(jnp.float32)
    middle_band = jnp.broadcast_to(line_coeff[:, None], (line_group, steps_all))
    solution = lax.linalg.tridiagonal_solve(
        below_band, middle_band, above_band, series[:, :, None]
    )[:, :, 0]
    blocked = solution.reshape(line_group, devices_tm, slabs)
    leading_next = jnp.concatenate(
        [solution[:, slabs::slabs], jnp.zeros((line_group, 1), jnp.float32)], axis=1
    )
    padded = jnp.concatenate([blocked, leading_next[:, :, None]], axis=2)
    returned = butterfly(jnp.transpose(padded, (1, 0, 2)), move_homeward)
    local_lines = returned.reshape(modes_local, count, slabs + 1)
    extended = jnp.transpose(local_lines, (0, 2, 1))
    phihat = extended[:, :slabs, :]
    left = lax.dynamic_slice(
        table, (mode_start, 0), (modes_local, rows_local * lax.axis_size("space"))
    )
    left_diff = lax.dynamic_slice(
        diff_table, (mode_start, 0), (modes_local, rows_local * lax.axis_size("space"))
    )
    values = jnp.einsum("ki,ktj->itj", left, extended, precision=highest)
    slopes = -jnp.einsum("ki,ktj->itj", left_diff, phihat, precision=highest)
    gathered = lax.psum_scatter(
        jnp.concatenate([values, slopes], axis=1), "space", scatter_dimension=0, tiled=True
    )
    physical = jnp.einsum("itk,kj->tij", gathered, table, precision=highest)
    potential = physical[: slabs + 1]
    grad_first = physical[slabs + 1 :]
    present = potential[:slabs]
    grad_second = jnp.concatenate(
        [present[:, :, 1:] - present[:, :, :-1], jnp.zeros_like(present[:, :, :1])], axis=2
    )
    density_out = rho - (present - potential[1:])
    flux_x_out = mom_x - flux_weight * grad_first
    flux_y_out = mom_y - flux_weight * grad_second
    return (density_out, flux_x_out, flux_y_out)


MESH = pl.DeviceIdType.MESH


def split_table(table):
    high = table.astype(jnp.bfloat16)
    low = (table - high.astype(np.float32)).astype(jnp.bfloat16)
    return np.stack([high, low], axis=-3)


def host_tables(count, parts, solvers):
    modes_local = count // parts
    modes = np.arange(count, dtype=np.float64)[:, None]
    points = np.arange(count, dtype=np.float64)[None, :]
    table = np.cos(np.pi * modes * (2.0 * points + 1.0) / (2.0 * count))
    table = table * np.where(modes == 0, np.sqrt(1.0 / count), np.sqrt(2.0 / count))
    wide = np.concatenate([table] + [table[:, -1:]] * 8, axis=1)
    forward, inverse, border = [], [], []
    for own in range(parts):
        mine = slice(own * modes_local, (own + 1) * modes_local)
        order = [own, 1 - own]
        forward.append(np.concatenate(
            [table[mine, q * modes_local:(q + 1) * modes_local] for q in order], axis=1))
        inverse.append(np.concatenate(
            [wide[mine, q * modes_local:(q + 1) * modes_local + 8].T for q in order[::-1]], axis=0))
        border.append(np.broadcast_to(
            -flux_weight * table[mine, modes_local:modes_local + 1], (modes_local, 128)))
    lam = 4.0 * np.sin(np.pi * np.arange(count) / (2.0 * count)) ** 2
    coeff = 2.0 + regular_shift + space_weight * (lam[:, None] + lam[None, :])
    rows = modes_local // solvers
    f32 = np.float32
    return (
        split_table(table.T.astype(f32)),
        split_table(table.astype(f32)),
        split_table(np.stack(forward).astype(f32)),
        split_table(np.stack(inverse).astype(f32)),
        np.stack(border).astype(f32),
        coeff.reshape(parts, solvers, rows, count).astype(f32),
    )


def parted(x):
    high = x.astype(jnp.bfloat16)
    return high, (x - high.astype(jnp.float32)).astype(jnp.bfloat16)


def mul(a, b):
    return jnp.dot(a, b, preferred_element_type=jnp.float32)


def by_table(x, table):
    high, low = parted(x)
    return mul(high, table[0]) + (mul(high, table[1]) + mul(low, table[0]))


def table_by(table, x):
    high, low = parted(x)
    return mul(table[0], high) + (mul(table[1], high) + mul(table[0], low))


def step_kernel(
    total, density, flux_x, flux_y, colf, coli, rowf, rowi, border, coeff,
    out_d, out_x, out_y,
    dv, xv, yv, rho, mx, my, colf_v, coli_v, rowf_v, rowi_v, border_v, coeff_v,
    stack, ysend, yrecv, outgoing, incoming, pivots, phi, home, psend, pown, precv,
    res_d, res_x, res_y,
    load_sem, ex_send, ex_recv, out_send, out_recv, back_send, back_recv, fin_send, fin_recv,
    store_sem,
):
    me = lax.axis_index("tm")
    side = lax.axis_index("space")
    rows, count = dv.shape
    group = coeff_v.shape[0]
    loads = [
        pltpu.make_async_copy(src, dst, load_sem.at[i])
        for i, (src, dst) in enumerate([
            (density.at[0], dv), (flux_x.at[0], xv), (flux_y.at[0], yv),
            (colf, colf_v), (rowf.at[side], rowf_v), (border.at[side], border_v),
            (coeff.at[side, me], coeff_v), (coli, coli_v), (rowi.at[side], rowi_v),
        ])
    ]
    for load in loads:
        load.start()
    near = sorted(range(1, total), key=lambda j: -min(j, total - j))
    peers = [lax.rem(me + j, total) for j in near]
    other = {"space": 1 - side}
    barrier = pltpu.get_barrier_semaphore()
    for peer in peers:
        pl.semaphore_signal(barrier, inc=1, device_id={"tm": peer}, device_id_type=MESH)
    pl.semaphore_signal(barrier, inc=1, device_id=other, device_id_type=MESH)

    for load in loads[:3]:
        load.wait()
    tile = 16

    def prox(i, carry):
        span = pl.ds(pl.multiple_of(i * tile, tile), tile)
        r, fx, fy = dv[span], xv[span], yv[span]
        q, a, b = kinetic_prox(r, fx, fy)
        rho[span] = q
        mx[span] = a
        my[span] = b
        return carry

    lax.fori_loop(0, rows // tile, prox, 0)
    loads[3].wait()

    def exchange(lo, size, k):
        span = pl.ds(lo, size)
        return pltpu.make_async_remote_copy(
            src_ref=ysend.at[span], dst_ref=yrecv.at[span], send_sem=ex_send.at[k],
            recv_sem=ex_recv.at[k], device_id=other, device_id_type=MESH)

    ysend[:rows] = by_table(rho[...], colf_v)
    pl.semaphore_wait(barrier, total)
    swap_rho = exchange(0, rows, 0)
    swap_rho.start()
    row = lax.broadcasted_iota(jnp.int32, (rows, count), 0)
    col = lax.broadcasted_iota(jnp.int32, (rows, count), 1)
    last = side * rows + row == 2 * rows - 1
    wx = jnp.where(last, 0.0, mx[...])
    wy = jnp.where(col == count - 1, 0.0, my[...])
    div = wx - jnp.where(row == 0, 0.0, pltpu.roll(wx, 1, 0)) + wy - pltpu.roll(wy, 1, 1)
    stack[:rows] = flux_weight * div
    stack[rows:] = wx[rows - 8:]
    ysend[rows:] = by_table(stack[...], colf_v)
    swap_div = exchange(rows, rows + 8, 1)
    swap_div.start()

    def outward(field, peer):
        return pltpu.make_async_remote_copy(
            src_ref=outgoing.at[field, peer], dst_ref=incoming.at[field, me],
            send_sem=out_send.at[field, peer], recv_sem=out_recv.at[field, me],
            device_id={"tm": peer}, device_id_type=MESH)

    def arrival(field, peer):
        return pltpu.make_async_remote_copy(
            src_ref=outgoing.at[field, peer], dst_ref=incoming.at[field, peer],
            send_sem=out_send.at[field, peer], recv_sem=out_recv.at[field, peer],
            device_id={"tm": peer}, device_id_type=MESH)

    loads[4].wait()
    loads[5].wait()
    swap_rho.wait_recv()
    both = jnp.concatenate([ysend[:rows], yrecv[:rows]], axis=0)
    outgoing[0] = table_by(rowf_v, both).reshape(total, group, count)
    for peer in peers:
        outward(0, peer).start()
    swap_div.wait_recv()
    both = jnp.concatenate([ysend[rows:2 * rows], yrecv[rows:2 * rows]], axis=0)
    halo = ysend[2 * rows + 7:2 * rows + 8] + yrecv[2 * rows + 7:2 * rows + 8]
    modal = table_by(rowf_v, both) + border_v[:, :1] * halo
    outgoing[1] = modal.reshape(total, group, count)
    for peer in peers:
        outward(1, peer).start()
    incoming[0, me] = outgoing[0, me]
    incoming[1, me] = outgoing[1, me]
    loads[6].wait()
    c = coeff_v[...]
    pivot = 1.0 / c
    pivots[0] = pivot
    for t in range(1, total):
        pivot = 1.0 / (c - pivot)
        pivots[t] = pivot
    for load in loads[7:]:
        load.wait()
    for peer in peers:
        arrival(0, peer).wait_recv()
        arrival(1, peer).wait_recv()
    phi[total] = jnp.zeros_like(c)
    value = (incoming[0, 0] + incoming[1, 0]) * pivots[0]
    phi[0] = value
    for t in range(1, total):
        value = (incoming[0, t] - incoming[0, t - 1] + incoming[1, t] + value) * pivots[t]
        phi[t] = value
    for t in reversed(range(total - 1)):
        value = phi[t] + pivots[t] * value
        phi[t] = value

    def homeward(peer, block):
        return pltpu.make_async_remote_copy(
            src_ref=phi.at[pl.ds(peer, 2)], dst_ref=home.at[block],
            send_sem=back_send.at[peer], recv_sem=back_recv.at[block],
            device_id={"tm": peer}, device_id_type=MESH)

    for peer in peers:
        homeward(peer, me).start()
    home[me, 0] = phi[me]
    home[me, 1] = phi[me + 1]
    for peer in peers:
        homeward(peer, peer).wait_recv()

    def final(k):
        return pltpu.make_async_remote_copy(
            src_ref=psend.at[k], dst_ref=precv.at[k], send_sem=fin_send.at[k],
            recv_sem=fin_recv.at[k], device_id=other, device_id_type=MESH)

    finals = [final(0), final(1)]
    for k in range(2):
        modes = home[:, k].reshape(rows, count)
        part = by_table(modes, coli_v)
        whole = table_by(rowi_v, part)
        psend[k] = whole[:rows + 8]
        finals[k].start()
        pown[k] = whole[rows + 8:]
    finals[0].wait_recv()
    pot = pown[0] + precv[0]
    here = pot[:rows]
    grad = pltpu.roll(pot, rows + 7, 0)[:rows] - here
    res_x[...] = mx[...] - flux_weight * grad
    save_x = pltpu.make_async_copy(res_x, out_x.at[0], store_sem.at[0])
    save_x.start()
    grad = jnp.where(col == count - 1, 0.0, pltpu.roll(here, count - 1, 1) - here)
    res_y[...] = my[...] - flux_weight * grad
    save_y = pltpu.make_async_copy(res_y, out_y.at[0], store_sem.at[1])
    save_y.start()
    finals[1].wait_recv()
    res_d[...] = rho[...] - (here - (pown[1, :rows] + precv[1, :rows]))
    save_d = pltpu.make_async_copy(res_d, out_d.at[0], store_sem.at[2])
    save_d.start()
    swap_rho.wait_send()
    swap_div.wait_send()
    for peer in peers:
        outward(0, peer).wait_send()
        outward(1, peer).wait_send()
        homeward(peer, me).wait_send()
    for copy in finals:
        copy.wait_send()
    for save in (save_x, save_y, save_d):
        save.wait()


def per_device_kernel(density, flux_x, flux_y):
    rows, count = density.shape[1:]
    parts = lax.axis_size("space")
    total = lax.axis_size("tm")
    group = rows // total
    tables = host_tables(count, parts, total)
    f32, bf16 = jnp.float32, jnp.bfloat16
    vm = pltpu.VMEM
    dma = pltpu.SemaphoreType.DMA
    slab = vm((rows, count), f32)
    scratch = [slab] * 6 + [
        vm((2, count, count), bf16), vm((2, count, count), bf16),
        vm((2, rows, count), bf16), vm((2, 2 * (rows + 8), rows), bf16),
        vm((rows, 128), f32), vm((group, count), f32),
        vm((rows + 8, count), f32), vm((2 * rows + 8, count), f32), vm((2 * rows + 8, count), f32),
        vm((2, total, group, count), f32), vm((2, total, group, count), f32),
        vm((total, group, count), f32), vm((total + 1, group, count), f32),
        vm((total, 2, group, count), f32),
        vm((2, rows + 8, count), f32), vm((2, rows + 8, count), f32), vm((2, rows + 8, count), f32),
        slab, slab, slab,
        dma((9,)), dma((2,)), dma((2,)), dma((2, total)), dma((2, total)),
        dma((total,)), dma((total,)), dma((2,)), dma((2,)), dma((3,)),
    ]
    anywhere = pl.BlockSpec(memory_space=pl.ANY)

    def kernel(*refs):
        step_kernel(total, *refs)

    return pl.pallas_call(
        kernel,
        out_shape=[jax.ShapeDtypeStruct(density.shape, f32)] * 3,
        in_specs=[anywhere] * 9,
        out_specs=[anywhere] * 3,
        scratch_shapes=scratch,
        compiler_params=pltpu.CompilerParams(collective_id=0, has_side_effects=True),
    )(density, flux_x, flux_y, *tables)


def per_device(density, flux_x, flux_y):
    slabs, rows, count = density.shape
    fits = slabs == 1 and lax.axis_size("space") == 2 and rows % (8 * lax.axis_size("tm")) == 0
    return (per_device_kernel if fits and count % 128 == 0 else per_device_xla)(
        density, flux_x, flux_y)


def solution(mesh):
    return jax.shard_map(
        per_device,
        mesh=mesh,
        in_specs=(P("tm", "space", None), P("tm", "space", None), P("tm", "space", None)),
        out_specs=(P("tm", "space", None), P("tm", "space", None), P("tm", "space", None)),
        check_vma=False,
    )
```

```python
import jax
import jax.numpy as jnp
import numpy as np
from jax import lax
from jax.experimental import pallas as pl
from jax.experimental.pallas import tpu as pltpu
from jax.sharding import PartitionSpec as P

NEWTON = 4


prox_weight = 1.0
regular_shift = 0.0001
space_weight = 0.25
flux_weight = 0.5
highest = lax.Precision.HIGHEST


def swapped(block, axis, distance):
    count = lax.axis_size(axis)
    route = []
    for low in range(count):
        high = low | 1 << distance
        if high != low and high < count:
            route += [(low, high), (high, low)]
    return lax.ppermute(block, axis, route)


def shifted(array, axis, by):
    size = lax.axis_size(axis)
    pairs = [(i, i + by) for i in range(size) if 0 <= i + by < size]
    return lax.ppermute(array, axis, pairs)


def kinetic_prox(density, flux_x, flux_y):
    square = flux_x * flux_x + flux_y * flux_y
    target = density + prox_weight + jnp.sqrt(square)
    for step in range(NEWTON):
        above = target + prox_weight
        value = (target - density) * above * above - 0.5 * prox_weight * square
        slope = above * (3.0 * target + prox_weight - 2.0 * density)
        target = target - value / slope
    shrink = target / (target + prox_weight)
    return (target, shrink * flux_x, shrink * flux_y)


def cosine_table(count):
    modes = jnp.arange(count).astype(jnp.float32)[:, None]
    points = jnp.arange(count).astype(jnp.float32)[None, :]
    table = jnp.cos(jnp.pi * modes * (2.0 * points + 1.0) / (2.0 * count))
    scales = jnp.where(modes == 0, jnp.sqrt(1.0 / count), jnp.sqrt(2.0 / count))
    return scales * table


def eigen_values(count):
    modes = jnp.arange(count).astype(jnp.float32)
    return 4.0 * jnp.sin(jnp.pi * modes / (2.0 * count)) ** 2


def move_outward(stacked, bit):
    return swapped(stacked, "tm", bit)


def move_homeward(stacked, bit):
    return swapped(stacked, "tm", bit)


def butterfly(blocks, mover):
    total = lax.axis_size("tm")
    position = lax.axis_index("tm")
    bit_count = total.bit_length() - 1
    for bit in range(bit_count):
        higher = total >> bit + 1
        lowest = 1 << bit
        shaped = blocks.reshape((higher, 2, lowest) + blocks.shape[1:])
        own_bit = position >> bit & 1
        keeping = jnp.where(own_bit == 0, shaped[:, 0], shaped[:, 1])
        leaving = jnp.where(own_bit == 0, shaped[:, 1], shaped[:, 0])
        arrived = mover(leaving, bit)
        first_half = jnp.where(own_bit == 0, keeping, arrived)
        second_half = jnp.where(own_bit == 0, arrived, keeping)
        blocks = jnp.stack([first_half, second_half], axis=1).reshape(blocks.shape)
    return blocks


def per_device_xla(density, flux_x, flux_y):
    slabs = density.shape[0]
    rows_local = density.shape[1]
    count = density.shape[2]
    parts = lax.axis_size("space")
    modes_local = count // parts
    own_start = lax.axis_index("space") * rows_local
    mode_start = lax.axis_index("space") * modes_local
    rho, mom_x, mom_y = kinetic_prox(density, flux_x, flux_y)
    prior = shifted(rho[slabs - 1], "tm", 1)
    before = jnp.concatenate([prior[None], rho[:-1]], axis=0)
    zeroed = mom_y.at[:, :, count - 1].set(0.0)
    div_second = zeroed - jnp.concatenate(
        [jnp.zeros_like(zeroed[:, :, :1]), zeroed[:, :, :-1]], axis=2
    )
    partial_source = rho - before + flux_weight * div_second
    table = cosine_table(count)
    diff_table = jnp.concatenate(
        [table[:, :-1] - table[:, 1:], jnp.zeros_like(table[:, :1])], axis=1
    )
    stacked = jnp.concatenate([partial_source, flux_weight * mom_x], axis=1)
    column_modes = jnp.einsum("tij,kj->itk", stacked, table, precision=highest)
    left = lax.dynamic_slice(
        table, (0, own_start), (modes_local * lax.axis_size("space"), rows_local)
    )
    left_diff = lax.dynamic_slice(
        diff_table, (0, own_start), (modes_local * lax.axis_size("space"), rows_local)
    )
    both = jnp.concatenate([left, left_diff], axis=1)
    modal = lax.psum_scatter(
        jnp.einsum("ki,itj->ktj", both, column_modes, precision=highest),
        "space",
        scatter_dimension=0,
        tiled=True,
    )
    lam = eigen_values(count)
    lam_local = lax.dynamic_slice_in_dim(lam, mode_start, modes_local)
    coeff = 2.0 + regular_shift + space_weight * (lam_local[:, None] + lam[None, :])
    devices_tm = lax.axis_size("tm")
    position = lax.axis_index("tm")
    lines_local = modes_local * count
    line_group = lines_local // devices_tm
    steps_all = devices_tm * slabs
    outgoing = jnp.transpose(modal, (0, 2, 1)).reshape(devices_tm, line_group, slabs)
    incoming = butterfly(outgoing, move_outward)
    series = jnp.transpose(incoming, (1, 0, 2)).reshape(line_group, steps_all)
    line_coeff = lax.dynamic_slice_in_dim(
        coeff.reshape(lines_local), position * line_group, line_group
    )
    column = lax.broadcasted_iota(jnp.int32, (line_group, steps_all), 1)
    below_band = jnp.where(column == 0, 0.0, -1.0).astype(jnp.float32)
    above_band = jnp.where(column == steps_all - 1, 0.0, -1.0).astype(jnp.float32)
    middle_band = jnp.broadcast_to(line_coeff[:, None], (line_group, steps_all))
    solution = lax.linalg.tridiagonal_solve(
        below_band, middle_band, above_band, series[:, :, None]
    )[:, :, 0]
    blocked = solution.reshape(line_group, devices_tm, slabs)
    leading_next = jnp.concatenate(
        [solution[:, slabs::slabs], jnp.zeros((line_group, 1), jnp.float32)], axis=1
    )
    padded = jnp.concatenate([blocked, leading_next[:, :, None]], axis=2)
    returned = butterfly(jnp.transpose(padded, (1, 0, 2)), move_homeward)
    local_lines = returned.reshape(modes_local, count, slabs + 1)
    extended = jnp.transpose(local_lines, (0, 2, 1))
    phihat = extended[:, :slabs, :]
    left = lax.dynamic_slice(
        table, (mode_start, 0), (modes_local, rows_local * lax.axis_size("space"))
    )
    left_diff = lax.dynamic_slice(
        diff_table, (mode_start, 0), (modes_local, rows_local * lax.axis_size("space"))
    )
    values = jnp.einsum("ki,ktj->itj", left, extended, precision=highest)
    slopes = -jnp.einsum("ki,ktj->itj", left_diff, phihat, precision=highest)
    gathered = lax.psum_scatter(
        jnp.concatenate([values, slopes], axis=1), "space", scatter_dimension=0, tiled=True
    )
    physical = jnp.einsum("itk,kj->tij", gathered, table, precision=highest)
    potential = physical[: slabs + 1]
    grad_first = physical[slabs + 1 :]
    present = potential[:slabs]
    grad_second = jnp.concatenate(
        [present[:, :, 1:] - present[:, :, :-1], jnp.zeros_like(present[:, :, :1])], axis=2
    )
    density_out = rho - (present - potential[1:])
    flux_x_out = mom_x - flux_weight * grad_first
    flux_y_out = mom_y - flux_weight * grad_second
    return (density_out, flux_x_out, flux_y_out)


MESH = pl.DeviceIdType.MESH


def split_table(table):
    high = table.astype(jnp.bfloat16)
    low = (table - high.astype(np.float32)).astype(jnp.bfloat16)
    return np.stack([high, low], axis=-3)


def host_tables(count, parts, solvers):
    modes_local = count // parts
    modes = np.arange(count, dtype=np.float64)[:, None]
    points = np.arange(count, dtype=np.float64)[None, :]
    table = np.cos(np.pi * modes * (2.0 * points + 1.0) / (2.0 * count))
    table = table * np.where(modes == 0, np.sqrt(1.0 / count), np.sqrt(2.0 / count))
    wide = np.concatenate([table] + [table[:, -1:]] * 8, axis=1)
    forward, inverse, border = [], [], []
    for own in range(parts):
        mine = slice(own * modes_local, (own + 1) * modes_local)
        order = [own, 1 - own]
        forward.append(np.concatenate(
            [table[mine, q * modes_local:(q + 1) * modes_local] for q in order], axis=1))
        inverse.append(np.concatenate(
            [wide[mine, q * modes_local:(q + 1) * modes_local + 8].T for q in order[::-1]], axis=0))
        border.append(np.broadcast_to(
            -flux_weight * table[mine, modes_local:modes_local + 1], (modes_local, 128)))
    lam = 4.0 * np.sin(np.pi * np.arange(count) / (2.0 * count)) ** 2
    coeff = 2.0 + regular_shift + space_weight * (lam[:, None] + lam[None, :])
    rows = modes_local // solvers
    f32 = np.float32
    return (
        split_table(table.T.astype(f32)),
        split_table(table.astype(f32)),
        split_table(np.stack(forward).astype(f32)),
        split_table(np.stack(inverse).astype(f32)),
        np.stack(border).astype(f32),
        coeff.reshape(parts, solvers, rows, count).astype(f32),
    )


def parted(x):
    high = x.astype(jnp.bfloat16)
    return high, (x - high.astype(jnp.float32)).astype(jnp.bfloat16)


def mul(a, b):
    return jnp.dot(a, b, preferred_element_type=jnp.float32)


def by_table(x, table):
    high, low = parted(x)
    return mul(high, table[0]) + (mul(high, table[1]) + mul(low, table[0]))


def table_by(table, x):
    high, low = parted(x)
    return mul(table[0], high) + (mul(table[1], high) + mul(table[0], low))


def step_kernel(
    total, density, flux_x, flux_y, colf, coli, rowf, rowi, border, coeff,
    rho, mx, my, pown, precv,
    dv, xv, yv, colf_v, coli_v, rowf_v, rowi_v, border_v, coeff_v,
    stack, ysend, yrecv, outgoing, incoming, pivots, phi, home, psend,
    load_sem, ex_send, ex_recv, out_send, out_recv, back_send, back_recv, fin_send, fin_recv,
):
    me = lax.axis_index("tm")
    side = lax.axis_index("space")
    rows, count = dv.shape
    group = coeff_v.shape[0]
    loads = [
        pltpu.make_async_copy(src, dst, load_sem.at[i])
        for i, (src, dst) in enumerate([
            (density.at[0], dv), (flux_x.at[0], xv), (flux_y.at[0], yv),
            (colf, colf_v), (rowf.at[side], rowf_v), (border.at[side], border_v),
            (coeff.at[side, me], coeff_v), (coli, coli_v), (rowi.at[side], rowi_v),
        ])
    ]
    for load in loads:
        load.start()
    near = sorted(range(1, total), key=lambda j: -min(j, total - j))
    peers = [lax.rem(me + j, total) for j in near]
    other = {"space": 1 - side}
    barrier = pltpu.get_barrier_semaphore()
    for peer in peers:
        pl.semaphore_signal(barrier, inc=1, device_id={"tm": peer}, device_id_type=MESH)
    pl.semaphore_signal(barrier, inc=1, device_id=other, device_id_type=MESH)

    for load in loads[:3]:
        load.wait()
    tile = 16

    def prox(i, carry):
        span = pl.ds(pl.multiple_of(i * tile, tile), tile)
        r, fx, fy = dv[span], xv[span], yv[span]
        q, a, b = kinetic_prox(r, fx, fy)
        rho[span] = q
        mx[span] = a
        my[span] = b
        return carry

    lax.fori_loop(0, rows // tile, prox, 0)
    loads[3].wait()

    def exchange(lo, size, k):
        span = pl.ds(lo, size)
        return pltpu.make_async_remote_copy(
            src_ref=ysend.at[span], dst_ref=yrecv.at[span], send_sem=ex_send.at[k],
            recv_sem=ex_recv.at[k], device_id=other, device_id_type=MESH)

    ysend[:rows] = by_table(rho[...], colf_v)
    pl.semaphore_wait(barrier, total)
    swap_rho = exchange(0, rows, 0)
    swap_rho.start()
    row = lax.broadcasted_iota(jnp.int32, (rows, count), 0)
    col = lax.broadcasted_iota(jnp.int32, (rows, count), 1)
    last = side * rows + row == 2 * rows - 1
    wx = jnp.where(last, 0.0, mx[...])
    wy = jnp.where(col == count - 1, 0.0, my[...])
    div = wx - jnp.where(row == 0, 0.0, pltpu.roll(wx, 1, 0)) + wy - pltpu.roll(wy, 1, 1)
    stack[:rows] = flux_weight * div
    stack[rows:] = wx[rows - 8:]
    ysend[rows:] = by_table(stack[...], colf_v)
    swap_div = exchange(rows, rows + 8, 1)
    swap_div.start()

    def outward(field, peer):
        return pltpu.make_async_remote_copy(
            src_ref=outgoing.at[field, peer], dst_ref=incoming.at[field, me],
            send_sem=out_send.at[field, peer], recv_sem=out_recv.at[field, me],
            device_id={"tm": peer}, device_id_type=MESH)

    def arrival(field, peer):
        return pltpu.make_async_remote_copy(
            src_ref=outgoing.at[field, peer], dst_ref=incoming.at[field, peer],
            send_sem=out_send.at[field, peer], recv_sem=out_recv.at[field, peer],
            device_id={"tm": peer}, device_id_type=MESH)

    loads[4].wait()
    loads[5].wait()
    swap_rho.wait_recv()
    both = jnp.concatenate([ysend[:rows], yrecv[:rows]], axis=0)
    outgoing[0] = table_by(rowf_v, both).reshape(total, group, count)
    for peer in peers:
        outward(0, peer).start()
    swap_div.wait_recv()
    both = jnp.concatenate([ysend[rows:2 * rows], yrecv[rows:2 * rows]], axis=0)
    halo = ysend[2 * rows + 7:2 * rows + 8] + yrecv[2 * rows + 7:2 * rows + 8]
    modal = table_by(rowf_v, both) + border_v[:, :1] * halo
    outgoing[1] = modal.reshape(total, group, count)
    for peer in peers:
        outward(1, peer).start()
    incoming[0, me] = outgoing[0, me]
    incoming[1, me] = outgoing[1, me]
    loads[6].wait()
    c = coeff_v[...]
    pivot = 1.0 / c
    pivots[0] = pivot
    for t in range(1, total):
        pivot = 1.0 / (c - pivot)
        pivots[t] = pivot
    for load in loads[7:]:
        load.wait()
    for peer in peers:
        arrival(0, peer).wait_recv()
        arrival(1, peer).wait_recv()
    phi[total] = jnp.zeros_like(c)
    value = (incoming[0, 0] + incoming[1, 0]) * pivots[0]
    phi[0] = value
    for t in range(1, total):
        value = (incoming[0, t] - incoming[0, t - 1] + incoming[1, t] + value) * pivots[t]
        phi[t] = value
    for t in reversed(range(total - 1)):
        value = phi[t] + pivots[t] * value
        phi[t] = value

    def homeward(peer, block):
        return pltpu.make_async_remote_copy(
            src_ref=phi.at[pl.ds(peer, 2)], dst_ref=home.at[block],
            send_sem=back_send.at[peer], recv_sem=back_recv.at[block],
            device_id={"tm": peer}, device_id_type=MESH)

    for peer in peers:
        homeward(peer, me).start()
    home[me, 0] = phi[me]
    home[me, 1] = phi[me + 1]
    for peer in peers:
        homeward(peer, peer).wait_recv()

    def final(k):
        return pltpu.make_async_remote_copy(
            src_ref=psend.at[k], dst_ref=precv.at[k], send_sem=fin_send.at[k],
            recv_sem=fin_recv.at[k], device_id=other, device_id_type=MESH)

    finals = [final(0), final(1)]
    for k in range(2):
        modes = home[:, k].reshape(rows, count)
        part = by_table(modes, coli_v)
        whole = table_by(rowi_v, part)
        psend[k] = whole[:rows + 8]
        finals[k].start()
        pown[k] = whole[rows + 8:]
    finals[0].wait_recv()
    finals[1].wait_recv()
    swap_rho.wait_send()
    swap_div.wait_send()
    for peer in peers:
        outward(0, peer).wait_send()
        outward(1, peer).wait_send()
        homeward(peer, me).wait_send()
    for copy in finals:
        copy.wait_send()


def finish_kernel(rho, mx, my, pown, precv, out_d, out_x, out_y, res_d, res_x, res_y, store_sem):
    rows, count = rho.shape
    col = lax.broadcasted_iota(jnp.int32, (rows, count), 1)
    pot = pown[0] + precv[0]
    here = pot[:rows]
    grad = pltpu.roll(pot, rows + 7, 0)[:rows] - here
    res_x[...] = mx[...] - flux_weight * grad
    save_x = pltpu.make_async_copy(res_x, out_x.at[0], store_sem.at[0])
    save_x.start()
    grad = jnp.where(col == count - 1, 0.0, pltpu.roll(here, count - 1, 1) - here)
    res_y[...] = my[...] - flux_weight * grad
    save_y = pltpu.make_async_copy(res_y, out_y.at[0], store_sem.at[1])
    save_y.start()
    res_d[...] = rho[...] - (here - (pown[1, :rows] + precv[1, :rows]))
    save_d = pltpu.make_async_copy(res_d, out_d.at[0], store_sem.at[2])
    save_d.start()
    for save in (save_x, save_y, save_d):
        save.wait()


def per_device_kernel(density, flux_x, flux_y):
    rows, count = density.shape[1:]
    parts = lax.axis_size("space")
    total = lax.axis_size("tm")
    group = rows // total
    tables = host_tables(count, parts, total)
    f32, bf16 = jnp.float32, jnp.bfloat16
    vm = pltpu.VMEM
    dma = pltpu.SemaphoreType.DMA
    slab = vm((rows, count), f32)
    scratch = [slab] * 3 + [
        vm((2, count, count), bf16), vm((2, count, count), bf16),
        vm((2, rows, count), bf16), vm((2, 2 * (rows + 8), rows), bf16),
        vm((rows, 128), f32), vm((group, count), f32),
        vm((rows + 8, count), f32), vm((2 * rows + 8, count), f32), vm((2 * rows + 8, count), f32),
        vm((2, total, group, count), f32), vm((2, total, group, count), f32),
        vm((total, group, count), f32), vm((total + 1, group, count), f32),
        vm((total, 2, group, count), f32),
        vm((2, rows + 8, count), f32),
        dma((9,)), dma((2,)), dma((2,)), dma((2, total)), dma((2, total)),
        dma((total,)), dma((total,)), dma((2,)), dma((2,)),
    ]
    anywhere = pl.BlockSpec(memory_space=pl.ANY)

    def kernel(*refs):
        step_kernel(total, *refs)

    local = pl.BlockSpec(memory_space=pltpu.VMEM)
    pair = vm((2, rows + 8, count), f32)
    held = pl.pallas_call(
        kernel,
        out_shape=[slab, slab, slab, pair, pair],
        in_specs=[anywhere] * 9,
        out_specs=[local] * 5,
        scratch_shapes=scratch,
        compiler_params=pltpu.CompilerParams(collective_id=0, has_side_effects=True),
    )(density, flux_x, flux_y, *tables)
    return pl.pallas_call(
        finish_kernel,
        out_shape=[jax.ShapeDtypeStruct(density.shape, f32)] * 3,
        in_specs=[local] * 5,
        out_specs=[anywhere] * 3,
        scratch_shapes=[slab, slab, slab, dma((3,))],
    )(*[pltpu.with_memory_space_constraint(x, pltpu.VMEM) for x in held])


def per_device(density, flux_x, flux_y):
    slabs, rows, count = density.shape
    fits = slabs == 1 and lax.axis_size("space") == 2 and rows % (8 * lax.axis_size("tm")) == 0
    return (per_device_kernel if fits and count % 128 == 0 else per_device_xla)(
        density, flux_x, flux_y)


def solution(mesh):
    return jax.shard_map(
        per_device,
        mesh=mesh,
        in_specs=(P("tm", "space", None), P("tm", "space", None), P("tm", "space", None)),
        out_specs=(P("tm", "space", None), P("tm", "space", None), P("tm", "space", None)),
        check_vma=False,
    )
```

```python
import jax
import jax.numpy as jnp
import numpy as np
from jax import lax
from jax.experimental import pallas as pl
from jax.experimental.pallas import tpu as pltpu
from jax.sharding import PartitionSpec as P

NEWTON = 4


prox_weight = 1.0
regular_shift = 0.0001
space_weight = 0.25
flux_weight = 0.5
highest = lax.Precision.HIGHEST


def swapped(block, axis, distance):
    count = lax.axis_size(axis)
    route = []
    for low in range(count):
        high = low | 1 << distance
        if high != low and high < count:
            route += [(low, high), (high, low)]
    return lax.ppermute(block, axis, route)


def shifted(array, axis, by):
    size = lax.axis_size(axis)
    pairs = [(i, i + by) for i in range(size) if 0 <= i + by < size]
    return lax.ppermute(array, axis, pairs)


def kinetic_prox(density, flux_x, flux_y):
    square = flux_x * flux_x + flux_y * flux_y
    target = density + prox_weight + jnp.sqrt(square)
    for step in range(NEWTON):
        above = target + prox_weight
        value = (target - density) * above * above - 0.5 * prox_weight * square
        slope = above * (3.0 * target + prox_weight - 2.0 * density)
        target = target - value / slope
    shrink = target / (target + prox_weight)
    return (target, shrink * flux_x, shrink * flux_y)


def cosine_table(count):
    modes = jnp.arange(count).astype(jnp.float32)[:, None]
    points = jnp.arange(count).astype(jnp.float32)[None, :]
    table = jnp.cos(jnp.pi * modes * (2.0 * points + 1.0) / (2.0 * count))
    scales = jnp.where(modes == 0, jnp.sqrt(1.0 / count), jnp.sqrt(2.0 / count))
    return scales * table


def eigen_values(count):
    modes = jnp.arange(count).astype(jnp.float32)
    return 4.0 * jnp.sin(jnp.pi * modes / (2.0 * count)) ** 2


def move_outward(stacked, bit):
    return swapped(stacked, "tm", bit)


def move_homeward(stacked, bit):
    return swapped(stacked, "tm", bit)


def butterfly(blocks, mover):
    total = lax.axis_size("tm")
    position = lax.axis_index("tm")
    bit_count = total.bit_length() - 1
    for bit in range(bit_count):
        higher = total >> bit + 1
        lowest = 1 << bit
        shaped = blocks.reshape((higher, 2, lowest) + blocks.shape[1:])
        own_bit = position >> bit & 1
        keeping = jnp.where(own_bit == 0, shaped[:, 0], shaped[:, 1])
        leaving = jnp.where(own_bit == 0, shaped[:, 1], shaped[:, 0])
        arrived = mover(leaving, bit)
        first_half = jnp.where(own_bit == 0, keeping, arrived)
        second_half = jnp.where(own_bit == 0, arrived, keeping)
        blocks = jnp.stack([first_half, second_half], axis=1).reshape(blocks.shape)
    return blocks


def per_device_xla(density, flux_x, flux_y):
    slabs = density.shape[0]
    rows_local = density.shape[1]
    count = density.shape[2]
    parts = lax.axis_size("space")
    modes_local = count // parts
    own_start = lax.axis_index("space") * rows_local
    mode_start = lax.axis_index("space") * modes_local
    rho, mom_x, mom_y = kinetic_prox(density, flux_x, flux_y)
    prior = shifted(rho[slabs - 1], "tm", 1)
    before = jnp.concatenate([prior[None], rho[:-1]], axis=0)
    zeroed = mom_y.at[:, :, count - 1].set(0.0)
    div_second = zeroed - jnp.concatenate(
        [jnp.zeros_like(zeroed[:, :, :1]), zeroed[:, :, :-1]], axis=2
    )
    partial_source = rho - before + flux_weight * div_second
    table = cosine_table(count)
    diff_table = jnp.concatenate(
        [table[:, :-1] - table[:, 1:], jnp.zeros_like(table[:, :1])], axis=1
    )
    stacked = jnp.concatenate([partial_source, flux_weight * mom_x], axis=1)
    column_modes = jnp.einsum("tij,kj->itk", stacked, table, precision=highest)
    left = lax.dynamic_slice(
        table, (0, own_start), (modes_local * lax.axis_size("space"), rows_local)
    )
    left_diff = lax.dynamic_slice(
        diff_table, (0, own_start), (modes_local * lax.axis_size("space"), rows_local)
    )
    both = jnp.concatenate([left, left_diff], axis=1)
    modal = lax.psum_scatter(
        jnp.einsum("ki,itj->ktj", both, column_modes, precision=highest),
        "space",
        scatter_dimension=0,
        tiled=True,
    )
    lam = eigen_values(count)
    lam_local = lax.dynamic_slice_in_dim(lam, mode_start, modes_local)
    coeff = 2.0 + regular_shift + space_weight * (lam_local[:, None] + lam[None, :])
    devices_tm = lax.axis_size("tm")
    position = lax.axis_index("tm")
    lines_local = modes_local * count
    line_group = lines_local // devices_tm
    steps_all = devices_tm * slabs
    outgoing = jnp.transpose(modal, (0, 2, 1)).reshape(devices_tm, line_group, slabs)
    incoming = butterfly(outgoing, move_outward)
    series = jnp.transpose(incoming, (1, 0, 2)).reshape(line_group, steps_all)
    line_coeff = lax.dynamic_slice_in_dim(
        coeff.reshape(lines_local), position * line_group, line_group
    )
    column = lax.broadcasted_iota(jnp.int32, (line_group, steps_all), 1)
    below_band = jnp.where(column == 0, 0.0, -1.0).astype(jnp.float32)
    above_band = jnp.where(column == steps_all - 1, 0.0, -1.0).astype(jnp.float32)
    middle_band = jnp.broadcast_to(line_coeff[:, None], (line_group, steps_all))
    solution = lax.linalg.tridiagonal_solve(
        below_band, middle_band, above_band, series[:, :, None]
    )[:, :, 0]
    blocked = solution.reshape(line_group, devices_tm, slabs)
    leading_next = jnp.concatenate(
        [solution[:, slabs::slabs], jnp.zeros((line_group, 1), jnp.float32)], axis=1
    )
    padded = jnp.concatenate([blocked, leading_next[:, :, None]], axis=2)
    returned = butterfly(jnp.transpose(padded, (1, 0, 2)), move_homeward)
    local_lines = returned.reshape(modes_local, count, slabs + 1)
    extended = jnp.transpose(local_lines, (0, 2, 1))
    phihat = extended[:, :slabs, :]
    left = lax.dynamic_slice(
        table, (mode_start, 0), (modes_local, rows_local * lax.axis_size("space"))
    )
    left_diff = lax.dynamic_slice(
        diff_table, (mode_start, 0), (modes_local, rows_local * lax.axis_size("space"))
    )
    values = jnp.einsum("ki,ktj->itj", left, extended, precision=highest)
    slopes = -jnp.einsum("ki,ktj->itj", left_diff, phihat, precision=highest)
    gathered = lax.psum_scatter(
        jnp.concatenate([values, slopes], axis=1), "space", scatter_dimension=0, tiled=True
    )
    physical = jnp.einsum("itk,kj->tij", gathered, table, precision=highest)
    potential = physical[: slabs + 1]
    grad_first = physical[slabs + 1 :]
    present = potential[:slabs]
    grad_second = jnp.concatenate(
        [present[:, :, 1:] - present[:, :, :-1], jnp.zeros_like(present[:, :, :1])], axis=2
    )
    density_out = rho - (present - potential[1:])
    flux_x_out = mom_x - flux_weight * grad_first
    flux_y_out = mom_y - flux_weight * grad_second
    return (density_out, flux_x_out, flux_y_out)


MESH = pl.DeviceIdType.MESH


def split_table(table):
    high = table.astype(jnp.bfloat16)
    low = (table - high.astype(np.float32)).astype(jnp.bfloat16)
    return np.stack([high, low], axis=-3)


def host_tables(count, parts, solvers):
    modes_local = count // parts
    modes = np.arange(count, dtype=np.float64)[:, None]
    points = np.arange(count, dtype=np.float64)[None, :]
    table = np.cos(np.pi * modes * (2.0 * points + 1.0) / (2.0 * count))
    table = table * np.where(modes == 0, np.sqrt(1.0 / count), np.sqrt(2.0 / count))
    wide = np.concatenate([table] + [table[:, -1:]] * 8, axis=1)
    forward, inverse, border = [], [], []
    for own in range(parts):
        mine = slice(own * modes_local, (own + 1) * modes_local)
        order = [own, 1 - own]
        forward.append(np.concatenate(
            [table[mine, q * modes_local:(q + 1) * modes_local] for q in order], axis=1))
        inverse.append(np.concatenate(
            [wide[mine, q * modes_local:(q + 1) * modes_local + 8].T for q in order[::-1]], axis=0))
        border.append(np.broadcast_to(
            -flux_weight * table[mine, modes_local:modes_local + 1], (modes_local, 128)))
    lam = 4.0 * np.sin(np.pi * np.arange(count) / (2.0 * count)) ** 2
    coeff = 2.0 + regular_shift + space_weight * (lam[:, None] + lam[None, :])
    rows = modes_local // solvers
    f32 = np.float32
    return (
        split_table(table.T.astype(f32)),
        split_table(table.astype(f32)),
        split_table(np.stack(forward).astype(f32)),
        split_table(np.stack(inverse).astype(f32)),
        np.stack(border).astype(f32),
        coeff.reshape(parts, solvers, rows, count).astype(f32),
    )


def parted(x):
    high = x.astype(jnp.bfloat16)
    return high, (x - high.astype(jnp.float32)).astype(jnp.bfloat16)


def mul(a, b):
    return jnp.dot(a, b, preferred_element_type=jnp.float32)


def by_table(x, table):
    high, low = parted(x)
    return mul(high, table[0]) + (mul(high, table[1]) + mul(low, table[0]))


def table_by(table, x):
    high, low = parted(x)
    return mul(table[0], high) + (mul(table[1], high) + mul(table[0], low))


def step_kernel(
    total, density, flux_x, flux_y, colf, coli, rowf, rowi, border, coeff,
    rho, mx, my, pown, precv,
    dv, xv, yv, colf_v, coli_v, rowf_v, rowi_v, border_v, coeff_v,
    stack, ysend, yrecv, outgoing, incoming, pivots, phi, home, psend, steps, cut,
    load_sem, ex_send, ex_recv, out_send, out_recv, back_send, back_recv, fin_send, fin_recv, cut_sem,
):
    place = lax.axis_index("tm")
    half = place // total
    me = place - half * total
    base = half * total
    mirror = {"tm": lax.rem(place + total, 2 * total)}
    side = lax.axis_index("space")
    rows, count = dv.shape
    group = coeff_v.shape[0]
    loads = [
        pltpu.make_async_copy(src, dst, load_sem.at[i])
        for i, (src, dst) in enumerate([
            (density.at[0], dv), (flux_x.at[0], xv), (flux_y.at[0], yv),
            (colf, colf_v), (rowf.at[side], rowf_v), (border.at[side], border_v),
            (coeff.at[side, me], coeff_v), (coli, coli_v), (rowi.at[side], rowi_v),
        ])
    ]
    for load in loads:
        load.start()
    near = sorted(range(1, total), key=lambda j: -min(j, total - j))
    peers = [lax.rem(me + j, total) for j in near]
    other = {"space": 1 - side}
    barrier = pltpu.get_barrier_semaphore()
    for peer in peers:
        pl.semaphore_signal(barrier, inc=1, device_id={"tm": base + peer}, device_id_type=MESH)
    pl.semaphore_signal(barrier, inc=1, device_id=mirror, device_id_type=MESH)
    pl.semaphore_signal(barrier, inc=1, device_id=other, device_id_type=MESH)

    for load in loads[:3]:
        load.wait()
    tile = 16

    def prox(i, carry):
        span = pl.ds(pl.multiple_of(i * tile, tile), tile)
        r, fx, fy = dv[span], xv[span], yv[span]
        q, a, b = kinetic_prox(r, fx, fy)
        rho[span] = q
        mx[span] = a
        my[span] = b
        return carry

    lax.fori_loop(0, rows // tile, prox, 0)
    loads[3].wait()

    def exchange(lo, size, k):
        span = pl.ds(lo, size)
        return pltpu.make_async_remote_copy(
            src_ref=ysend.at[span], dst_ref=yrecv.at[span], send_sem=ex_send.at[k],
            recv_sem=ex_recv.at[k], device_id=other, device_id_type=MESH)

    ysend[:rows] = by_table(rho[...], colf_v)
    pl.semaphore_wait(barrier, total + 1)
    swap_rho = exchange(0, rows, 0)
    swap_rho.start()
    row = lax.broadcasted_iota(jnp.int32, (rows, count), 0)
    col = lax.broadcasted_iota(jnp.int32, (rows, count), 1)
    last = side * rows + row == 2 * rows - 1
    wx = jnp.where(last, 0.0, mx[...])
    wy = jnp.where(col == count - 1, 0.0, my[...])
    div = wx - jnp.where(row == 0, 0.0, pltpu.roll(wx, 1, 0)) + wy - pltpu.roll(wy, 1, 1)
    stack[:rows] = flux_weight * div
    stack[rows:] = wx[rows - 8:]
    ysend[rows:] = by_table(stack[...], colf_v)
    swap_div = exchange(rows, rows + 8, 1)
    swap_div.start()

    def outward(field, peer):
        return pltpu.make_async_remote_copy(
            src_ref=outgoing.at[field, peer], dst_ref=incoming.at[field, me],
            send_sem=out_send.at[field, peer], recv_sem=out_recv.at[field, me],
            device_id={"tm": base + peer}, device_id_type=MESH)

    def arrival(field, peer):
        return pltpu.make_async_remote_copy(
            src_ref=outgoing.at[field, peer], dst_ref=incoming.at[field, peer],
            send_sem=out_send.at[field, peer], recv_sem=out_recv.at[field, peer],
            device_id={"tm": base + peer}, device_id_type=MESH)

    loads[4].wait()
    loads[5].wait()
    swap_rho.wait_recv()
    both = jnp.concatenate([ysend[:rows], yrecv[:rows]], axis=0)
    outgoing[0] = table_by(rowf_v, both).reshape(total, group, count)
    for peer in peers:
        outward(0, peer).start()
    swap_div.wait_recv()
    both = jnp.concatenate([ysend[rows:2 * rows], yrecv[rows:2 * rows]], axis=0)
    halo = ysend[2 * rows + 7:2 * rows + 8] + yrecv[2 * rows + 7:2 * rows + 8]
    modal = table_by(rowf_v, both) + border_v[:, :1] * halo
    outgoing[1] = modal.reshape(total, group, count)
    for peer in peers:
        outward(1, peer).start()
    incoming[0, me] = outgoing[0, me]
    incoming[1, me] = outgoing[1, me]
    loads[6].wait()
    c = coeff_v[...]
    pivot = 1.0 / c
    pivots[0] = pivot
    for t in range(1, total):
        pivot = 1.0 / (c - pivot)
        pivots[t] = pivot
    inverse = 1.0 / (1.0 - pivot * pivot)
    for load in loads[7:]:
        load.wait()
    for peer in peers:
        arrival(0, peer).wait_recv()
        arrival(1, peer).wait_recv()
    right = jnp.full(c.shape, half, jnp.int32) == 1
    start, stride = half * (total - 1), 1 - 2 * half
    steps[0] = incoming[0, 0] + incoming[1, 0]
    for t in range(1, total):
        steps[t] = incoming[0, t] - incoming[0, t - 1] + incoming[1, t]
    value = jnp.zeros_like(c)
    for i in range(total):
        value = (steps[start + stride * i] + value) * pivots[i]
        steps[start + stride * i] = value
    edge = jnp.where(right, 0.0, incoming[0, total - 1])
    cut[0] = value - edge
    swap = pltpu.make_async_remote_copy(
        src_ref=cut.at[0], dst_ref=cut.at[1], send_sem=cut_sem.at[0], recv_sem=cut_sem.at[1],
        device_id=mirror, device_id_type=MESH)
    swap.start()
    swap.wait_recv()
    beyond = cut[1] - pivot * edge
    value = (value + pivot * beyond) * inverse
    phi[total] = jnp.where(right, 0.0, beyond + pivot * value)
    phi[start + stride * (total - 1)] = value
    for i in reversed(range(total - 1)):
        value = steps[start + stride * i] + pivots[i] * value
        phi[start + stride * i] = value

    def homeward(peer, block):
        return pltpu.make_async_remote_copy(
            src_ref=phi.at[pl.ds(peer, 2)], dst_ref=home.at[block],
            send_sem=back_send.at[peer], recv_sem=back_recv.at[block],
            device_id={"tm": base + peer}, device_id_type=MESH)

    for peer in peers:
        homeward(peer, me).start()
    home[me, 0] = phi[me]
    home[me, 1] = phi[me + 1]
    for peer in peers:
        homeward(peer, peer).wait_recv()

    def final(k):
        return pltpu.make_async_remote_copy(
            src_ref=psend.at[k], dst_ref=precv.at[k], send_sem=fin_send.at[k],
            recv_sem=fin_recv.at[k], device_id=other, device_id_type=MESH)

    finals = [final(0), final(1)]
    for k in range(2):
        modes = home[:, k].reshape(rows, count)
        part = by_table(modes, coli_v)
        whole = table_by(rowi_v, part)
        psend[k] = whole[:rows + 8]
        finals[k].start()
        pown[k] = whole[rows + 8:]
    finals[0].wait_recv()
    finals[1].wait_recv()
    swap_rho.wait_send()
    swap_div.wait_send()
    for peer in peers:
        outward(0, peer).wait_send()
        outward(1, peer).wait_send()
        homeward(peer, me).wait_send()
    for copy in finals:
        copy.wait_send()
    swap.wait_send()


def finish_kernel(rho, mx, my, pown, precv, out_d, out_x, out_y, res_d, res_x, res_y, store_sem):
    rows, count = rho.shape
    col = lax.broadcasted_iota(jnp.int32, (rows, count), 1)
    pot = pown[0] + precv[0]
    here = pot[:rows]
    grad = pltpu.roll(pot, rows + 7, 0)[:rows] - here
    res_x[...] = mx[...] - flux_weight * grad
    save_x = pltpu.make_async_copy(res_x, out_x.at[0], store_sem.at[0])
    save_x.start()
    grad = jnp.where(col == count - 1, 0.0, pltpu.roll(here, count - 1, 1) - here)
    res_y[...] = my[...] - flux_weight * grad
    save_y = pltpu.make_async_copy(res_y, out_y.at[0], store_sem.at[1])
    save_y.start()
    res_d[...] = rho[...] - (here - (pown[1, :rows] + precv[1, :rows]))
    save_d = pltpu.make_async_copy(res_d, out_d.at[0], store_sem.at[2])
    save_d.start()
    for save in (save_x, save_y, save_d):
        save.wait()


def per_device_kernel(density, flux_x, flux_y):
    rows, count = density.shape[1:]
    parts = lax.axis_size("space")
    total = lax.axis_size("tm") // 2
    group = rows // total
    tables = host_tables(count, parts, total)
    f32, bf16 = jnp.float32, jnp.bfloat16
    vm = pltpu.VMEM
    dma = pltpu.SemaphoreType.DMA
    slab = vm((rows, count), f32)
    scratch = [slab] * 3 + [
        vm((2, count, count), bf16), vm((2, count, count), bf16),
        vm((2, rows, count), bf16), vm((2, 2 * (rows + 8), rows), bf16),
        vm((rows, 128), f32), vm((group, count), f32),
        vm((rows + 8, count), f32), vm((2 * rows + 8, count), f32), vm((2 * rows + 8, count), f32),
        vm((2, total, group, count), f32), vm((2, total, group, count), f32),
        vm((total, group, count), f32), vm((total + 1, group, count), f32),
        vm((total, 2, group, count), f32),
        vm((2, rows + 8, count), f32), vm((total, group, count), f32), vm((2, group, count), f32),
        dma((9,)), dma((2,)), dma((2,)), dma((2, total)), dma((2, total)),
        dma((total,)), dma((total,)), dma((2,)), dma((2,)), dma((2,)),
    ]
    anywhere = pl.BlockSpec(memory_space=pl.ANY)

    def kernel(*refs):
        step_kernel(total, *refs)

    local = pl.BlockSpec(memory_space=pltpu.VMEM)
    pair = vm((2, rows + 8, count), f32)
    held = pl.pallas_call(
        kernel,
        out_shape=[slab, slab, slab, pair, pair],
        in_specs=[anywhere] * 9,
        out_specs=[local] * 5,
        scratch_shapes=scratch,
        compiler_params=pltpu.CompilerParams(collective_id=0, has_side_effects=True),
    )(density, flux_x, flux_y, *tables)
    return pl.pallas_call(
        finish_kernel,
        out_shape=[jax.ShapeDtypeStruct(density.shape, f32)] * 3,
        in_specs=[local] * 5,
        out_specs=[anywhere] * 3,
        scratch_shapes=[slab, slab, slab, dma((3,))],
    )(*[pltpu.with_memory_space_constraint(x, pltpu.VMEM) for x in held])


def per_device(density, flux_x, flux_y):
    slabs, rows, count = density.shape
    size = lax.axis_size("tm")
    fits = slabs == 1 and lax.axis_size("space") == 2 and size % 2 == 0 and rows % (4 * size) == 0
    return (per_device_kernel if fits and count % 128 == 0 else per_device_xla)(
        density, flux_x, flux_y)


def solution(mesh):
    return jax.shard_map(
        per_device,
        mesh=mesh,
        in_specs=(P("tm", "space", None), P("tm", "space", None), P("tm", "space", None)),
        out_specs=(P("tm", "space", None), P("tm", "space", None), P("tm", "space", None)),
        check_vma=False,
    )
```

```python
import jax
import jax.numpy as jnp
import numpy as np
from jax import lax
from jax.experimental import pallas as pl
from jax.experimental.pallas import tpu as pltpu
from jax.sharding import PartitionSpec as P

NEWTON = 4


prox_weight = 1.0
regular_shift = 0.0001
space_weight = 0.25
flux_weight = 0.5
highest = lax.Precision.HIGHEST


def swapped(block, axis, distance):
    count = lax.axis_size(axis)
    route = []
    for low in range(count):
        high = low | 1 << distance
        if high != low and high < count:
            route += [(low, high), (high, low)]
    return lax.ppermute(block, axis, route)


def shifted(array, axis, by):
    size = lax.axis_size(axis)
    pairs = [(i, i + by) for i in range(size) if 0 <= i + by < size]
    return lax.ppermute(array, axis, pairs)


def kinetic_prox(density, flux_x, flux_y):
    square = flux_x * flux_x + flux_y * flux_y
    target = density + prox_weight + jnp.sqrt(square)
    for step in range(NEWTON):
        above = target + prox_weight
        value = (target - density) * above * above - 0.5 * prox_weight * square
        slope = above * (3.0 * target + prox_weight - 2.0 * density)
        target = target - value / slope
    shrink = target / (target + prox_weight)
    return (target, shrink * flux_x, shrink * flux_y)


def cosine_table(count):
    modes = jnp.arange(count).astype(jnp.float32)[:, None]
    points = jnp.arange(count).astype(jnp.float32)[None, :]
    table = jnp.cos(jnp.pi * modes * (2.0 * points + 1.0) / (2.0 * count))
    scales = jnp.where(modes == 0, jnp.sqrt(1.0 / count), jnp.sqrt(2.0 / count))
    return scales * table


def eigen_values(count):
    modes = jnp.arange(count).astype(jnp.float32)
    return 4.0 * jnp.sin(jnp.pi * modes / (2.0 * count)) ** 2


def move_outward(stacked, bit):
    return swapped(stacked, "tm", bit)


def move_homeward(stacked, bit):
    return swapped(stacked, "tm", bit)


def butterfly(blocks, mover):
    total = lax.axis_size("tm")
    position = lax.axis_index("tm")
    bit_count = total.bit_length() - 1
    for bit in range(bit_count):
        higher = total >> bit + 1
        lowest = 1 << bit
        shaped = blocks.reshape((higher, 2, lowest) + blocks.shape[1:])
        own_bit = position >> bit & 1
        keeping = jnp.where(own_bit == 0, shaped[:, 0], shaped[:, 1])
        leaving = jnp.where(own_bit == 0, shaped[:, 1], shaped[:, 0])
        arrived = mover(leaving, bit)
        first_half = jnp.where(own_bit == 0, keeping, arrived)
        second_half = jnp.where(own_bit == 0, arrived, keeping)
        blocks = jnp.stack([first_half, second_half], axis=1).reshape(blocks.shape)
    return blocks


def per_device_xla(density, flux_x, flux_y):
    slabs = density.shape[0]
    rows_local = density.shape[1]
    count = density.shape[2]
    parts = lax.axis_size("space")
    modes_local = count // parts
    own_start = lax.axis_index("space") * rows_local
    mode_start = lax.axis_index("space") * modes_local
    rho, mom_x, mom_y = kinetic_prox(density, flux_x, flux_y)
    prior = shifted(rho[slabs - 1], "tm", 1)
    before = jnp.concatenate([prior[None], rho[:-1]], axis=0)
    zeroed = mom_y.at[:, :, count - 1].set(0.0)
    div_second = zeroed - jnp.concatenate(
        [jnp.zeros_like(zeroed[:, :, :1]), zeroed[:, :, :-1]], axis=2
    )
    partial_source = rho - before + flux_weight * div_second
    table = cosine_table(count)
    diff_table = jnp.concatenate(
        [table[:, :-1] - table[:, 1:], jnp.zeros_like(table[:, :1])], axis=1
    )
    stacked = jnp.concatenate([partial_source, flux_weight * mom_x], axis=1)
    column_modes = jnp.einsum("tij,kj->itk", stacked, table, precision=highest)
    left = lax.dynamic_slice(
        table, (0, own_start), (modes_local * lax.axis_size("space"), rows_local)
    )
    left_diff = lax.dynamic_slice(
        diff_table, (0, own_start), (modes_local * lax.axis_size("space"), rows_local)
    )
    both = jnp.concatenate([left, left_diff], axis=1)
    modal = lax.psum_scatter(
        jnp.einsum("ki,itj->ktj", both, column_modes, precision=highest),
        "space",
        scatter_dimension=0,
        tiled=True,
    )
    lam = eigen_values(count)
    lam_local = lax.dynamic_slice_in_dim(lam, mode_start, modes_local)
    coeff = 2.0 + regular_shift + space_weight * (lam_local[:, None] + lam[None, :])
    devices_tm = lax.axis_size("tm")
    position = lax.axis_index("tm")
    lines_local = modes_local * count
    line_group = lines_local // devices_tm
    steps_all = devices_tm * slabs
    outgoing = jnp.transpose(modal, (0, 2, 1)).reshape(devices_tm, line_group, slabs)
    incoming = butterfly(outgoing, move_outward)
    series = jnp.transpose(incoming, (1, 0, 2)).reshape(line_group, steps_all)
    line_coeff = lax.dynamic_slice_in_dim(
        coeff.reshape(lines_local), position * line_group, line_group
    )
    column = lax.broadcasted_iota(jnp.int32, (line_group, steps_all), 1)
    below_band = jnp.where(column == 0, 0.0, -1.0).astype(jnp.float32)
    above_band = jnp.where(column == steps_all - 1, 0.0, -1.0).astype(jnp.float32)
    middle_band = jnp.broadcast_to(line_coeff[:, None], (line_group, steps_all))
    solution = lax.linalg.tridiagonal_solve(
        below_band, middle_band, above_band, series[:, :, None]
    )[:, :, 0]
    blocked = solution.reshape(line_group, devices_tm, slabs)
    leading_next = jnp.concatenate(
        [solution[:, slabs::slabs], jnp.zeros((line_group, 1), jnp.float32)], axis=1
    )
    padded = jnp.concatenate([blocked, leading_next[:, :, None]], axis=2)
    returned = butterfly(jnp.transpose(padded, (1, 0, 2)), move_homeward)
    local_lines = returned.reshape(modes_local, count, slabs + 1)
    extended = jnp.transpose(local_lines, (0, 2, 1))
    phihat = extended[:, :slabs, :]
    left = lax.dynamic_slice(
        table, (mode_start, 0), (modes_local, rows_local * lax.axis_size("space"))
    )
    left_diff = lax.dynamic_slice(
        diff_table, (mode_start, 0), (modes_local, rows_local * lax.axis_size("space"))
    )
    values = jnp.einsum("ki,ktj->itj", left, extended, precision=highest)
    slopes = -jnp.einsum("ki,ktj->itj", left_diff, phihat, precision=highest)
    gathered = lax.psum_scatter(
        jnp.concatenate([values, slopes], axis=1), "space", scatter_dimension=0, tiled=True
    )
    physical = jnp.einsum("itk,kj->tij", gathered, table, precision=highest)
    potential = physical[: slabs + 1]
    grad_first = physical[slabs + 1 :]
    present = potential[:slabs]
    grad_second = jnp.concatenate(
        [present[:, :, 1:] - present[:, :, :-1], jnp.zeros_like(present[:, :, :1])], axis=2
    )
    density_out = rho - (present - potential[1:])
    flux_x_out = mom_x - flux_weight * grad_first
    flux_y_out = mom_y - flux_weight * grad_second
    return (density_out, flux_x_out, flux_y_out)


MESH = pl.DeviceIdType.MESH
CHUNKS = 2


def split_table(table):
    high = table.astype(jnp.bfloat16)
    low = (table - high.astype(np.float32)).astype(jnp.bfloat16)
    return np.stack([high, low], axis=-3)


def host_tables(count, parts, solvers):
    modes_local = count // parts
    modes = np.arange(count, dtype=np.float64)[:, None]
    points = np.arange(count, dtype=np.float64)[None, :]
    table = np.cos(np.pi * modes * (2.0 * points + 1.0) / (2.0 * count))
    table = table * np.where(modes == 0, np.sqrt(1.0 / count), np.sqrt(2.0 / count))
    wide = np.concatenate([table] + [table[:, -1:]] * 8, axis=1)
    forward, inverse, border = [], [], []
    for own in range(parts):
        mine = slice(own * modes_local, (own + 1) * modes_local)
        order = [own, 1 - own]
        forward.append(np.concatenate(
            [table[mine, q * modes_local:(q + 1) * modes_local] for q in order], axis=1))
        inverse.append(np.concatenate(
            [wide[q * modes_local:(q + 1) * modes_local,
                  own * modes_local:(own + 1) * modes_local + 8].T for q in order], axis=1))
        border.append(np.broadcast_to(
            -flux_weight * table[mine, modes_local:modes_local + 1], (modes_local, 128)))
    lam = 4.0 * np.sin(np.pi * np.arange(count) / (2.0 * count)) ** 2
    coeff = 2.0 + regular_shift + space_weight * (lam[:, None] + lam[None, :])
    rows = modes_local // solvers
    f32 = np.float32
    return (
        split_table(table.T.astype(f32)),
        split_table(table.astype(f32)),
        split_table(np.stack(forward).astype(f32)),
        split_table(np.stack(inverse).astype(f32)),
        np.stack(border).astype(f32),
        coeff.reshape(parts, solvers, rows, count).astype(f32),
    )


def parted(x):
    high = x.astype(jnp.bfloat16)
    return high, (x - high.astype(jnp.float32)).astype(jnp.bfloat16)


def mul(a, b):
    return jnp.dot(a, b, preferred_element_type=jnp.float32)


def by_table(x, table):
    high, low = parted(x)
    return mul(high, table[0]) + (mul(high, table[1]) + mul(low, table[0]))


def table_by(table, x):
    high, low = parted(x)
    return mul(table[0], high) + (mul(table[1], high) + mul(table[0], low))


def step_kernel(
    total, density, flux_x, flux_y, colf, coli, rowf, rowi, border, coeff,
    rho, mx, my, fields,
    dv, xv, yv, colf_v, coli_v, rowf_v, rowi_v, border_v, coeff_v,
    stack, ysend, yrecv, outgoing, incoming, pivots, phi, home, across, steps, cut,
    load_sem, ex_send, ex_recv, out_send, out_recv, back_send, back_recv, fin_send, fin_recv, cut_sem,
):
    place = lax.axis_index("tm")
    half = place // total
    me = place - half * total
    base = half * total
    mirror = {"tm": lax.rem(place + total, 2 * total)}
    side = lax.axis_index("space")
    rows, count = dv.shape
    group = coeff_v.shape[0]
    part = group // CHUNKS
    loads = [
        pltpu.make_async_copy(src, dst, load_sem.at[i])
        for i, (src, dst) in enumerate([
            (density.at[0], dv), (flux_x.at[0], xv), (flux_y.at[0], yv),
            (colf, colf_v), (rowf.at[side], rowf_v), (border.at[side], border_v),
            (coeff.at[side, me], coeff_v), (coli, coli_v), (rowi.at[side], rowi_v),
        ])
    ]
    for load in loads:
        load.start()
    near = sorted(range(1, total), key=lambda j: -min(j, total - j))
    peers = [lax.rem(me + j, total) for j in near]
    other = {"space": 1 - side}
    barrier = pltpu.get_barrier_semaphore()
    for peer in peers:
        pl.semaphore_signal(barrier, inc=1, device_id={"tm": base + peer}, device_id_type=MESH)
    pl.semaphore_signal(barrier, inc=1, device_id=mirror, device_id_type=MESH)
    pl.semaphore_signal(barrier, inc=1, device_id=other, device_id_type=MESH)

    for load in loads[:3]:
        load.wait()
    tile = 16

    def prox(i, carry):
        span = pl.ds(pl.multiple_of(i * tile, tile), tile)
        r, fx, fy = dv[span], xv[span], yv[span]
        q, a, b = kinetic_prox(r, fx, fy)
        rho[span] = q
        mx[span] = a
        my[span] = b
        return carry

    lax.fori_loop(0, rows // tile, prox, 0)
    loads[3].wait()

    def exchange(lo, size, k):
        span = pl.ds(lo, size)
        return pltpu.make_async_remote_copy(
            src_ref=ysend.at[span], dst_ref=yrecv.at[span], send_sem=ex_send.at[k],
            recv_sem=ex_recv.at[k], device_id=other, device_id_type=MESH)

    ysend[:rows] = by_table(rho[...], colf_v)
    pl.semaphore_wait(barrier, total + 1)
    swap_rho = exchange(0, rows, 0)
    swap_rho.start()
    row = lax.broadcasted_iota(jnp.int32, (rows, count), 0)
    col = lax.broadcasted_iota(jnp.int32, (rows, count), 1)
    last = side * rows + row == 2 * rows - 1
    wx = jnp.where(last, 0.0, mx[...])
    wy = jnp.where(col == count - 1, 0.0, my[...])
    div = wx - jnp.where(row == 0, 0.0, pltpu.roll(wx, 1, 0)) + wy - pltpu.roll(wy, 1, 1)
    stack[:rows] = flux_weight * div
    stack[rows:] = wx[rows - 8:]
    ysend[rows:] = by_table(stack[...], colf_v)
    swap_div = exchange(rows, rows + 8, 1)
    swap_div.start()

    def outward(field, k, peer):
        span = pl.ds(k * part, part)
        return pltpu.make_async_remote_copy(
            src_ref=outgoing.at[field, peer, span], dst_ref=incoming.at[field, me, span],
            send_sem=out_send.at[field, k, peer], recv_sem=out_recv.at[field, k, me],
            device_id={"tm": base + peer}, device_id_type=MESH)

    def arrival(field, k, peer):
        span = pl.ds(k * part, part)
        return pltpu.make_async_remote_copy(
            src_ref=outgoing.at[field, peer, span], dst_ref=incoming.at[field, peer, span],
            send_sem=out_send.at[field, k, peer], recv_sem=out_recv.at[field, k, peer],
            device_id={"tm": base + peer}, device_id_type=MESH)

    loads[4].wait()
    loads[5].wait()
    swap_rho.wait_recv()
    both = jnp.concatenate([ysend[:rows], yrecv[:rows]], axis=0)
    outgoing[0] = table_by(rowf_v, both).reshape(total, group, count)
    for peer in peers:
        outward(0, 0, peer).start()
    swap_div.wait_recv()
    both = jnp.concatenate([ysend[rows:2 * rows], yrecv[rows:2 * rows]], axis=0)
    halo = ysend[2 * rows + 7:2 * rows + 8] + yrecv[2 * rows + 7:2 * rows + 8]
    modal = table_by(rowf_v, both) + border_v[:, :1] * halo
    outgoing[1] = modal.reshape(total, group, count)
    for field, k in ((1, 0), (0, 1), (1, 1)):
        for peer in peers:
            outward(field, k, peer).start()
    incoming[0, me] = outgoing[0, me]
    incoming[1, me] = outgoing[1, me]
    loads[6].wait()
    c = coeff_v[...]
    pivot = 1.0 / c
    pivots[0] = pivot
    for t in range(1, total):
        pivot = 1.0 / (c - pivot)
        pivots[t] = pivot
    inverse = 1.0 / (1.0 - pivot * pivot)
    for load in loads[7:]:
        load.wait()
    right = jnp.full((part, count), half, jnp.int32) == 1
    start, stride = half * (total - 1), 1 - 2 * half

    def swap(k):
        return pltpu.make_async_remote_copy(
            src_ref=cut.at[0, k], dst_ref=cut.at[1, k], send_sem=cut_sem.at[0, k],
            recv_sem=cut_sem.at[1, k], device_id=mirror, device_id_type=MESH)

    def homeward(k, peer, block):
        return pltpu.make_async_remote_copy(
            src_ref=phi.at[k, pl.ds(peer, 2)], dst_ref=home.at[k, block],
            send_sem=back_send.at[k, peer], recv_sem=back_recv.at[k, block],
            device_id={"tm": base + peer}, device_id_type=MESH)

    def relay(k, block):
        return pltpu.make_async_remote_copy(
            src_ref=home.at[k, block], dst_ref=across.at[k, block],
            send_sem=fin_send.at[k, block], recv_sem=fin_recv.at[k, block],
            device_id=other, device_id_type=MESH)

    ends = []
    for k in range(CHUNKS):
        span = slice(k * part, (k + 1) * part)
        for peer in reversed(peers):
            arrival(0, k, peer).wait_recv()
            arrival(1, k, peer).wait_recv()
        steps[0, span] = incoming[0, 0, span] + incoming[1, 0, span]
        for t in range(1, total):
            steps[t, span] = (
                incoming[0, t, span] - incoming[0, t - 1, span] + incoming[1, t, span])
        value = jnp.zeros((part, count), jnp.float32)
        for i in range(total):
            value = (steps[start + stride * i, span] + value) * pivots[i, span]
            steps[start + stride * i, span] = value
        edge = jnp.where(right, 0.0, incoming[0, total - 1, span])
        cut[0, k] = value - edge
        swap(k).start()
        ends.append((value, edge))
    for k in range(CHUNKS):
        span = slice(k * part, (k + 1) * part)
        value, edge = ends[k]
        swap(k).wait_recv()
        pivot = pivots[total - 1, span]
        beyond = cut[1, k] - pivot * edge
        value = (value + pivot * beyond) * inverse[span]
        phi[k, total] = jnp.where(right, 0.0, beyond + pivot * value)
        phi[k, start + stride * (total - 1)] = value
        for i in reversed(range(total - 1)):
            value = steps[start + stride * i, span] + pivots[i, span] * value
            phi[k, start + stride * i] = value
        for peer in peers:
            homeward(k, peer, me).start()
        home[k, me, 0] = phi[k, me]
        home[k, me, 1] = phi[k, me + 1]
        relay(k, me).start()
    for k in range(CHUNKS):
        for peer in reversed(peers):
            homeward(k, peer, peer).wait_recv()
            relay(k, peer).start()
    for k in range(CHUNKS):
        for block in [me] + peers:
            relay(k, block).wait_recv()

    def modes(ref, field):
        return jnp.concatenate(
            [ref[k, block, field] for block in range(total) for k in range(CHUNKS)], axis=0)

    for field in range(2):
        both = jnp.concatenate([modes(home, field), modes(across, field)], axis=0)
        fields[field] = by_table(table_by(rowi_v, both), coli_v)
    swap_rho.wait_send()
    swap_div.wait_send()
    for k in range(CHUNKS):
        swap(k).wait_send()
        relay(k, me).wait_send()
        for peer in peers:
            outward(0, k, peer).wait_send()
            outward(1, k, peer).wait_send()
            homeward(k, peer, me).wait_send()
            relay(k, peer).wait_send()


def finish_kernel(rho, mx, my, fields, out_d, out_x, out_y, res_d, res_x, res_y, store_sem):
    rows, count = rho.shape
    col = lax.broadcasted_iota(jnp.int32, (rows, count), 1)
    pot = fields[0]
    here = pot[:rows]
    grad = pltpu.roll(pot, rows + 7, 0)[:rows] - here
    res_x[...] = mx[...] - flux_weight * grad
    save_x = pltpu.make_async_copy(res_x, out_x.at[0], store_sem.at[0])
    save_x.start()
    grad = jnp.where(col == count - 1, 0.0, pltpu.roll(here, count - 1, 1) - here)
    res_y[...] = my[...] - flux_weight * grad
    save_y = pltpu.make_async_copy(res_y, out_y.at[0], store_sem.at[1])
    save_y.start()
    res_d[...] = rho[...] - (here - fields[1, :rows])
    save_d = pltpu.make_async_copy(res_d, out_d.at[0], store_sem.at[2])
    save_d.start()
    for save in (save_x, save_y, save_d):
        save.wait()


def per_device_kernel(density, flux_x, flux_y):
    rows, count = density.shape[1:]
    parts = lax.axis_size("space")
    total = lax.axis_size("tm") // 2
    group = rows // total
    part = group // CHUNKS
    tables = host_tables(count, parts, total)
    f32, bf16 = jnp.float32, jnp.bfloat16
    vm = pltpu.VMEM
    dma = pltpu.SemaphoreType.DMA
    slab = vm((rows, count), f32)
    scratch = [slab] * 3 + [
        vm((2, count, count), bf16), vm((2, count, count), bf16),
        vm((2, rows, count), bf16), vm((2, rows + 8, count), bf16),
        vm((rows, 128), f32), vm((group, count), f32),
        vm((rows + 8, count), f32), vm((2 * rows + 8, count), f32), vm((2 * rows + 8, count), f32),
        vm((2, total, group, count), f32), vm((2, total, group, count), f32),
        vm((total, group, count), f32), vm((CHUNKS, total + 1, part, count), f32),
        vm((CHUNKS, total, 2, part, count), f32), vm((CHUNKS, total, 2, part, count), f32),
        vm((total, group, count), f32), vm((2, CHUNKS, part, count), f32),
        dma((9,)), dma((2,)), dma((2,)), dma((2, CHUNKS, total)), dma((2, CHUNKS, total)),
        dma((CHUNKS, total)), dma((CHUNKS, total)), dma((CHUNKS, total)), dma((CHUNKS, total)),
        dma((2, CHUNKS)),
    ]
    anywhere = pl.BlockSpec(memory_space=pl.ANY)

    def kernel(*refs):
        step_kernel(total, *refs)

    local = pl.BlockSpec(memory_space=pltpu.VMEM)
    pair = vm((2, rows + 8, count), f32)
    held = pl.pallas_call(
        kernel,
        out_shape=[slab, slab, slab, pair],
        in_specs=[anywhere] * 9,
        out_specs=[local] * 4,
        scratch_shapes=scratch,
        compiler_params=pltpu.CompilerParams(collective_id=0, has_side_effects=True),
    )(density, flux_x, flux_y, *tables)
    return pl.pallas_call(
        finish_kernel,
        out_shape=[jax.ShapeDtypeStruct(density.shape, f32)] * 3,
        in_specs=[local] * 4,
        out_specs=[anywhere] * 3,
        scratch_shapes=[slab, slab, slab, dma((3,))],
    )(*[pltpu.with_memory_space_constraint(x, pltpu.VMEM) for x in held])


def per_device(density, flux_x, flux_y):
    slabs, rows, count = density.shape
    size = lax.axis_size("tm")
    fits = slabs == 1 and lax.axis_size("space") == 2 and size % 2 == 0 and rows % (4 * CHUNKS * size) == 0
    return (per_device_kernel if fits and count % 128 == 0 else per_device_xla)(
        density, flux_x, flux_y)


def solution(mesh):
    return jax.shard_map(
        per_device,
        mesh=mesh,
        in_specs=(P("tm", "space", None), P("tm", "space", None), P("tm", "space", None)),
        out_specs=(P("tm", "space", None), P("tm", "space", None), P("tm", "space", None)),
        check_vma=False,
    )
```

```python
import jax
import jax.numpy as jnp
import numpy as np
from jax import lax
from jax.experimental import pallas as pl
from jax.experimental.pallas import tpu as pltpu
from jax.sharding import PartitionSpec as P

NEWTON = 4


prox_weight = 1.0
regular_shift = 0.0001
space_weight = 0.25
flux_weight = 0.5
highest = lax.Precision.HIGHEST


def swapped(block, axis, distance):
    count = lax.axis_size(axis)
    route = []
    for low in range(count):
        high = low | 1 << distance
        if high != low and high < count:
            route += [(low, high), (high, low)]
    return lax.ppermute(block, axis, route)


def shifted(array, axis, by):
    size = lax.axis_size(axis)
    pairs = [(i, i + by) for i in range(size) if 0 <= i + by < size]
    return lax.ppermute(array, axis, pairs)


def kinetic_prox(density, flux_x, flux_y):
    square = flux_x * flux_x + flux_y * flux_y
    target = density + prox_weight + jnp.sqrt(square)
    for step in range(NEWTON):
        above = target + prox_weight
        value = (target - density) * above * above - 0.5 * prox_weight * square
        slope = above * (3.0 * target + prox_weight - 2.0 * density)
        target = target - value / slope
    shrink = target / (target + prox_weight)
    return (target, shrink * flux_x, shrink * flux_y)


def cosine_table(count):
    modes = jnp.arange(count).astype(jnp.float32)[:, None]
    points = jnp.arange(count).astype(jnp.float32)[None, :]
    table = jnp.cos(jnp.pi * modes * (2.0 * points + 1.0) / (2.0 * count))
    scales = jnp.where(modes == 0, jnp.sqrt(1.0 / count), jnp.sqrt(2.0 / count))
    return scales * table


def eigen_values(count):
    modes = jnp.arange(count).astype(jnp.float32)
    return 4.0 * jnp.sin(jnp.pi * modes / (2.0 * count)) ** 2


def move_outward(stacked, bit):
    return swapped(stacked, "tm", bit)


def move_homeward(stacked, bit):
    return swapped(stacked, "tm", bit)


def butterfly(blocks, mover):
    total = lax.axis_size("tm")
    position = lax.axis_index("tm")
    bit_count = total.bit_length() - 1
    for bit in range(bit_count):
        higher = total >> bit + 1
        lowest = 1 << bit
        shaped = blocks.reshape((higher, 2, lowest) + blocks.shape[1:])
        own_bit = position >> bit & 1
        keeping = jnp.where(own_bit == 0, shaped[:, 0], shaped[:, 1])
        leaving = jnp.where(own_bit == 0, shaped[:, 1], shaped[:, 0])
        arrived = mover(leaving, bit)
        first_half = jnp.where(own_bit == 0, keeping, arrived)
        second_half = jnp.where(own_bit == 0, arrived, keeping)
        blocks = jnp.stack([first_half, second_half], axis=1).reshape(blocks.shape)
    return blocks


def per_device_xla(density, flux_x, flux_y):
    slabs = density.shape[0]
    rows_local = density.shape[1]
    count = density.shape[2]
    parts = lax.axis_size("space")
    modes_local = count // parts
    own_start = lax.axis_index("space") * rows_local
    mode_start = lax.axis_index("space") * modes_local
    rho, mom_x, mom_y = kinetic_prox(density, flux_x, flux_y)
    prior = shifted(rho[slabs - 1], "tm", 1)
    before = jnp.concatenate([prior[None], rho[:-1]], axis=0)
    zeroed = mom_y.at[:, :, count - 1].set(0.0)
    div_second = zeroed - jnp.concatenate(
        [jnp.zeros_like(zeroed[:, :, :1]), zeroed[:, :, :-1]], axis=2
    )
    partial_source = rho - before + flux_weight * div_second
    table = cosine_table(count)
    diff_table = jnp.concatenate(
        [table[:, :-1] - table[:, 1:], jnp.zeros_like(table[:, :1])], axis=1
    )
    stacked = jnp.concatenate([partial_source, flux_weight * mom_x], axis=1)
    column_modes = jnp.einsum("tij,kj->itk", stacked, table, precision=highest)
    left = lax.dynamic_slice(
        table, (0, own_start), (modes_local * lax.axis_size("space"), rows_local)
    )
    left_diff = lax.dynamic_slice(
        diff_table, (0, own_start), (modes_local * lax.axis_size("space"), rows_local)
    )
    both = jnp.concatenate([left, left_diff], axis=1)
    modal = lax.psum_scatter(
        jnp.einsum("ki,itj->ktj", both, column_modes, precision=highest),
        "space",
        scatter_dimension=0,
        tiled=True,
    )
    lam = eigen_values(count)
    lam_local = lax.dynamic_slice_in_dim(lam, mode_start, modes_local)
    coeff = 2.0 + regular_shift + space_weight * (lam_local[:, None] + lam[None, :])
    devices_tm = lax.axis_size("tm")
    position = lax.axis_index("tm")
    lines_local = modes_local * count
    line_group = lines_local // devices_tm
    steps_all = devices_tm * slabs
    outgoing = jnp.transpose(modal, (0, 2, 1)).reshape(devices_tm, line_group, slabs)
    incoming = butterfly(outgoing, move_outward)
    series = jnp.transpose(incoming, (1, 0, 2)).reshape(line_group, steps_all)
    line_coeff = lax.dynamic_slice_in_dim(
        coeff.reshape(lines_local), position * line_group, line_group
    )
    column = lax.broadcasted_iota(jnp.int32, (line_group, steps_all), 1)
    below_band = jnp.where(column == 0, 0.0, -1.0).astype(jnp.float32)
    above_band = jnp.where(column == steps_all - 1, 0.0, -1.0).astype(jnp.float32)
    middle_band = jnp.broadcast_to(line_coeff[:, None], (line_group, steps_all))
    solution = lax.linalg.tridiagonal_solve(
        below_band, middle_band, above_band, series[:, :, None]
    )[:, :, 0]
    blocked = solution.reshape(line_group, devices_tm, slabs)
    leading_next = jnp.concatenate(
        [solution[:, slabs::slabs], jnp.zeros((line_group, 1), jnp.float32)], axis=1
    )
    padded = jnp.concatenate([blocked, leading_next[:, :, None]], axis=2)
    returned = butterfly(jnp.transpose(padded, (1, 0, 2)), move_homeward)
    local_lines = returned.reshape(modes_local, count, slabs + 1)
    extended = jnp.transpose(local_lines, (0, 2, 1))
    phihat = extended[:, :slabs, :]
    left = lax.dynamic_slice(
        table, (mode_start, 0), (modes_local, rows_local * lax.axis_size("space"))
    )
    left_diff = lax.dynamic_slice(
        diff_table, (mode_start, 0), (modes_local, rows_local * lax.axis_size("space"))
    )
    values = jnp.einsum("ki,ktj->itj", left, extended, precision=highest)
    slopes = -jnp.einsum("ki,ktj->itj", left_diff, phihat, precision=highest)
    gathered = lax.psum_scatter(
        jnp.concatenate([values, slopes], axis=1), "space", scatter_dimension=0, tiled=True
    )
    physical = jnp.einsum("itk,kj->tij", gathered, table, precision=highest)
    potential = physical[: slabs + 1]
    grad_first = physical[slabs + 1 :]
    present = potential[:slabs]
    grad_second = jnp.concatenate(
        [present[:, :, 1:] - present[:, :, :-1], jnp.zeros_like(present[:, :, :1])], axis=2
    )
    density_out = rho - (present - potential[1:])
    flux_x_out = mom_x - flux_weight * grad_first
    flux_y_out = mom_y - flux_weight * grad_second
    return (density_out, flux_x_out, flux_y_out)


MESH = pl.DeviceIdType.MESH
CHUNKS = 2


def split_table(table):
    high = table.astype(jnp.bfloat16)
    low = (table - high.astype(np.float32)).astype(jnp.bfloat16)
    return np.stack([high, low], axis=-3)


def host_tables(count, parts, solvers):
    modes_local = count // parts
    modes = np.arange(count, dtype=np.float64)[:, None]
    points = np.arange(count, dtype=np.float64)[None, :]
    table = np.cos(np.pi * modes * (2.0 * points + 1.0) / (2.0 * count))
    table = table * np.where(modes == 0, np.sqrt(1.0 / count), np.sqrt(2.0 / count))
    wide = np.concatenate([table] + [table[:, -1:]] * 8, axis=1)
    forward, inverse, border = [], [], []
    for own in range(parts):
        mine = slice(own * modes_local, (own + 1) * modes_local)
        order = [own, 1 - own]
        forward.append(np.concatenate(
            [table[mine, q * modes_local:(q + 1) * modes_local] for q in order], axis=1))
        inverse.append(np.concatenate(
            [wide[q * modes_local:(q + 1) * modes_local,
                  own * modes_local:(own + 1) * modes_local + 8].T for q in order], axis=1))
        border.append(np.broadcast_to(
            -flux_weight * table[mine, modes_local:modes_local + 1], (modes_local, 128)))
    lam = 4.0 * np.sin(np.pi * np.arange(count) / (2.0 * count)) ** 2
    coeff = 2.0 + regular_shift + space_weight * (lam[:, None] + lam[None, :])
    rows = modes_local // solvers
    f32 = np.float32
    return (
        split_table(table.T.astype(f32)),
        split_table(table.astype(f32)),
        split_table(np.stack(forward).astype(f32)),
        split_table(np.stack(inverse).astype(f32)),
        np.stack(border).astype(f32),
        coeff.reshape(parts, solvers, rows, count).astype(f32),
    )


def parted(x):
    high = x.astype(jnp.bfloat16)
    return high, (x - high.astype(jnp.float32)).astype(jnp.bfloat16)


def mul(a, b):
    return jnp.dot(a, b, preferred_element_type=jnp.float32)


def by_table(x, table):
    high, low = parted(x)
    return mul(high, table[0]) + (mul(high, table[1]) + mul(low, table[0]))


def table_by(table, x):
    high, low = parted(x)
    return mul(table[0], high) + (mul(table[1], high) + mul(table[0], low))


def step_kernel(
    total, density, flux_x, flux_y, colf, coli, rowf, rowi, border, coeff,
    rho, mx, my, fields,
    dv, xv, yv, colf_v, coli_v, rowf_v, rowi_v, border_v, coeff_v,
    stack, ysend, yrecv, outgoing, incoming, pivots, phi, home, across, steps, cut,
    load_sem, ex_send, ex_recv, out_send, out_recv, back_send, back_recv, fin_send, fin_recv, cut_sem,
):
    place = lax.axis_index("tm")
    half = place // total
    me = place - half * total
    base = half * total
    mirror = {"tm": lax.rem(place + total, 2 * total)}
    side = lax.axis_index("space")
    rows, count = dv.shape
    group = coeff_v.shape[0]
    part = group // CHUNKS
    loads = [
        pltpu.make_async_copy(src, dst, load_sem.at[i])
        for i, (src, dst) in enumerate([
            (density.at[0], dv), (flux_x.at[0], xv), (flux_y.at[0], yv),
            (colf, colf_v), (rowf.at[side], rowf_v), (border.at[side], border_v),
            (coeff.at[side, me], coeff_v), (coli, coli_v), (rowi.at[side], rowi_v),
        ])
    ]
    for load in loads:
        load.start()
    bits = [1 << i for i in range(total.bit_length() - 1)]
    flips = [bit * (1 - 2 * lax.rem(me // bit, 2)) for bit in bits]
    masks = sorted(range(1, total), key=lambda m: (-bin(m).count("1"), -m))
    peers = [me + sum(f for f, bit in zip(flips, bits) if m & bit) for m in masks]
    other = {"space": 1 - side}
    barrier = pltpu.get_barrier_semaphore()
    for peer in peers:
        pl.semaphore_signal(barrier, inc=1, device_id={"tm": base + peer}, device_id_type=MESH)
    pl.semaphore_signal(barrier, inc=1, device_id=mirror, device_id_type=MESH)
    pl.semaphore_signal(barrier, inc=1, device_id=other, device_id_type=MESH)

    for load in loads[:3]:
        load.wait()
    tile = 16

    def prox(i, carry):
        span = pl.ds(pl.multiple_of(i * tile, tile), tile)
        r, fx, fy = dv[span], xv[span], yv[span]
        q, a, b = kinetic_prox(r, fx, fy)
        rho[span] = q
        mx[span] = a
        my[span] = b
        return carry

    lax.fori_loop(0, rows // tile, prox, 0)
    loads[3].wait()

    def exchange(lo, size, k):
        span = pl.ds(lo, size)
        return pltpu.make_async_remote_copy(
            src_ref=ysend.at[span], dst_ref=yrecv.at[span], send_sem=ex_send.at[k],
            recv_sem=ex_recv.at[k], device_id=other, device_id_type=MESH)

    ysend[:rows] = by_table(rho[...], colf_v)
    pl.semaphore_wait(barrier, total + 1)
    swap_rho = exchange(0, rows, 0)
    swap_rho.start()
    row = lax.broadcasted_iota(jnp.int32, (rows, count), 0)
    col = lax.broadcasted_iota(jnp.int32, (rows, count), 1)
    last = side * rows + row == 2 * rows - 1
    wx = jnp.where(last, 0.0, mx[...])
    wy = jnp.where(col == count - 1, 0.0, my[...])
    div = wx - jnp.where(row == 0, 0.0, pltpu.roll(wx, 1, 0)) + wy - pltpu.roll(wy, 1, 1)
    stack[:rows] = flux_weight * div
    stack[rows:] = wx[rows - 8:]
    ysend[rows:] = by_table(stack[...], colf_v)
    swap_div = exchange(rows, rows + 8, 1)
    swap_div.start()

    def outward(field, k, peer):
        span = pl.ds(k * part, part)
        return pltpu.make_async_remote_copy(
            src_ref=outgoing.at[field, peer, span], dst_ref=incoming.at[field, me, span],
            send_sem=out_send.at[field, k, peer], recv_sem=out_recv.at[field, k, me],
            device_id={"tm": base + peer}, device_id_type=MESH)

    def arrival(field, k, peer):
        span = pl.ds(k * part, part)
        return pltpu.make_async_remote_copy(
            src_ref=outgoing.at[field, peer, span], dst_ref=incoming.at[field, peer, span],
            send_sem=out_send.at[field, k, peer], recv_sem=out_recv.at[field, k, peer],
            device_id={"tm": base + peer}, device_id_type=MESH)

    loads[4].wait()
    loads[5].wait()
    swap_rho.wait_recv()
    both = jnp.concatenate([ysend[:rows], yrecv[:rows]], axis=0)
    outgoing[0] = table_by(rowf_v, both).reshape(total, group, count)
    for peer in peers:
        outward(0, 0, peer).start()
    swap_div.wait_recv()
    both = jnp.concatenate([ysend[rows:2 * rows], yrecv[rows:2 * rows]], axis=0)
    halo = ysend[2 * rows + 7:2 * rows + 8] + yrecv[2 * rows + 7:2 * rows + 8]
    modal = table_by(rowf_v, both) + border_v[:, :1] * halo
    outgoing[1] = modal.reshape(total, group, count)
    for field, k in ((1, 0), (0, 1), (1, 1)):
        for peer in peers:
            outward(field, k, peer).start()
    incoming[0, me] = outgoing[0, me]
    incoming[1, me] = outgoing[1, me]
    loads[6].wait()
    c = coeff_v[...]
    pivot = 1.0 / c
    pivots[0] = pivot
    for t in range(1, total):
        pivot = 1.0 / (c - pivot)
        pivots[t] = pivot
    inverse = 1.0 / (1.0 - pivot * pivot)
    for load in loads[7:]:
        load.wait()
    right = jnp.full((part, count), half, jnp.int32) == 1
    start, stride = half * (total - 1), 1 - 2 * half

    def swap(k):
        return pltpu.make_async_remote_copy(
            src_ref=cut.at[0, k], dst_ref=cut.at[1, k], send_sem=cut_sem.at[0, k],
            recv_sem=cut_sem.at[1, k], device_id=mirror, device_id_type=MESH)

    def homeward(k, peer, block):
        return pltpu.make_async_remote_copy(
            src_ref=phi.at[k, pl.ds(peer, 2)], dst_ref=home.at[k, block],
            send_sem=back_send.at[k, peer], recv_sem=back_recv.at[k, block],
            device_id={"tm": base + peer}, device_id_type=MESH)

    def relay(k, block):
        return pltpu.make_async_remote_copy(
            src_ref=home.at[k, block], dst_ref=across.at[k, block],
            send_sem=fin_send.at[k, block], recv_sem=fin_recv.at[k, block],
            device_id=other, device_id_type=MESH)

    ends = []
    for k in range(CHUNKS):
        span = slice(k * part, (k + 1) * part)
        for peer in reversed(peers):
            arrival(0, k, peer).wait_recv()
            arrival(1, k, peer).wait_recv()
        steps[0, span] = incoming[0, 0, span] + incoming[1, 0, span]
        for t in range(1, total):
            steps[t, span] = (
                incoming[0, t, span] - incoming[0, t - 1, span] + incoming[1, t, span])
        value = jnp.zeros((part, count), jnp.float32)
        for i in range(total):
            value = (steps[start + stride * i, span] + value) * pivots[i, span]
            steps[start + stride * i, span] = value
        edge = jnp.where(right, 0.0, incoming[0, total - 1, span])
        cut[0, k] = value - edge
        swap(k).start()
        ends.append((value, edge))
    for k in range(CHUNKS):
        span = slice(k * part, (k + 1) * part)
        value, edge = ends[k]
        swap(k).wait_recv()
        pivot = pivots[total - 1, span]
        beyond = cut[1, k] - pivot * edge
        value = (value + pivot * beyond) * inverse[span]
        phi[k, total] = jnp.where(right, 0.0, beyond + pivot * value)
        phi[k, start + stride * (total - 1)] = value
        for i in reversed(range(total - 1)):
            value = steps[start + stride * i, span] + pivots[i, span] * value
            phi[k, start + stride * i] = value
        for peer in peers:
            homeward(k, peer, me).start()
        home[k, me, 0] = phi[k, me]
        home[k, me, 1] = phi[k, me + 1]
        relay(k, me).start()
    for k in range(CHUNKS):
        for peer in reversed(peers):
            homeward(k, peer, peer).wait_recv()
            relay(k, peer).start()
    for k in range(CHUNKS):
        for block in [me] + peers:
            relay(k, block).wait_recv()

    def modes(ref, field):
        return jnp.concatenate(
            [ref[k, block, field] for block in range(total) for k in range(CHUNKS)], axis=0)

    for field in range(2):
        both = jnp.concatenate([modes(home, field), modes(across, field)], axis=0)
        fields[field] = by_table(table_by(rowi_v, both), coli_v)
    swap_rho.wait_send()
    swap_div.wait_send()
    for k in range(CHUNKS):
        swap(k).wait_send()
        relay(k, me).wait_send()
        for peer in peers:
            outward(0, k, peer).wait_send()
            outward(1, k, peer).wait_send()
            homeward(k, peer, me).wait_send()
            relay(k, peer).wait_send()


def finish_kernel(rho, mx, my, fields, out_d, out_x, out_y, res_d, res_x, res_y, store_sem):
    rows, count = rho.shape
    col = lax.broadcasted_iota(jnp.int32, (rows, count), 1)
    pot = fields[0]
    here = pot[:rows]
    grad = pltpu.roll(pot, rows + 7, 0)[:rows] - here
    res_x[...] = mx[...] - flux_weight * grad
    save_x = pltpu.make_async_copy(res_x, out_x.at[0], store_sem.at[0])
    save_x.start()
    grad = jnp.where(col == count - 1, 0.0, pltpu.roll(here, count - 1, 1) - here)
    res_y[...] = my[...] - flux_weight * grad
    save_y = pltpu.make_async_copy(res_y, out_y.at[0], store_sem.at[1])
    save_y.start()
    res_d[...] = rho[...] - (here - fields[1, :rows])
    save_d = pltpu.make_async_copy(res_d, out_d.at[0], store_sem.at[2])
    save_d.start()
    for save in (save_x, save_y, save_d):
        save.wait()


def per_device_kernel(density, flux_x, flux_y):
    rows, count = density.shape[1:]
    parts = lax.axis_size("space")
    total = lax.axis_size("tm") // 2
    group = rows // total
    part = group // CHUNKS
    tables = host_tables(count, parts, total)
    f32, bf16 = jnp.float32, jnp.bfloat16
    vm = pltpu.VMEM
    dma = pltpu.SemaphoreType.DMA
    slab = vm((rows, count), f32)
    scratch = [slab] * 3 + [
        vm((2, count, count), bf16), vm((2, count, count), bf16),
        vm((2, rows, count), bf16), vm((2, rows + 8, count), bf16),
        vm((rows, 128), f32), vm((group, count), f32),
        vm((rows + 8, count), f32), vm((2 * rows + 8, count), f32), vm((2 * rows + 8, count), f32),
        vm((2, total, group, count), f32), vm((2, total, group, count), f32),
        vm((total, group, count), f32), vm((CHUNKS, total + 1, part, count), f32),
        vm((CHUNKS, total, 2, part, count), f32), vm((CHUNKS, total, 2, part, count), f32),
        vm((total, group, count), f32), vm((2, CHUNKS, part, count), f32),
        dma((9,)), dma((2,)), dma((2,)), dma((2, CHUNKS, total)), dma((2, CHUNKS, total)),
        dma((CHUNKS, total)), dma((CHUNKS, total)), dma((CHUNKS, total)), dma((CHUNKS, total)),
        dma((2, CHUNKS)),
    ]
    anywhere = pl.BlockSpec(memory_space=pl.ANY)

    def kernel(*refs):
        step_kernel(total, *refs)

    local = pl.BlockSpec(memory_space=pltpu.VMEM)
    pair = vm((2, rows + 8, count), f32)
    held = pl.pallas_call(
        kernel,
        out_shape=[slab, slab, slab, pair],
        in_specs=[anywhere] * 9,
        out_specs=[local] * 4,
        scratch_shapes=scratch,
        compiler_params=pltpu.CompilerParams(collective_id=0, has_side_effects=True),
    )(density, flux_x, flux_y, *tables)
    return pl.pallas_call(
        finish_kernel,
        out_shape=[jax.ShapeDtypeStruct(density.shape, f32)] * 3,
        in_specs=[local] * 4,
        out_specs=[anywhere] * 3,
        scratch_shapes=[slab, slab, slab, dma((3,))],
    )(*[pltpu.with_memory_space_constraint(x, pltpu.VMEM) for x in held])


def per_device(density, flux_x, flux_y):
    slabs, rows, count = density.shape
    size = lax.axis_size("tm")
    fits = slabs == 1 and lax.axis_size("space") == 2 and size % 2 == 0 and rows % (4 * CHUNKS * size) == 0 and size & (size - 1) == 0
    return (per_device_kernel if fits and count % 128 == 0 else per_device_xla)(
        density, flux_x, flux_y)


def solution(mesh):
    return jax.shard_map(
        per_device,
        mesh=mesh,
        in_specs=(P("tm", "space", None), P("tm", "space", None), P("tm", "space", None)),
        out_specs=(P("tm", "space", None), P("tm", "space", None), P("tm", "space", None)),
        check_vma=False,
    )
```
